128 devices in a mesh: lat: 8 (over x, core), lon: 16 (over y, z).
Axes of the slice: x: 4, y: 4, z: 4, core: 2. Of those that a mesh axis runs over, the one named last changes fastest.
Arguments:
- adjoint_in: float32 [16, 72, 64, 2048], P(None, None, 'lat', 'lon'), may hold values from -6 to 6
- horiz_frac: float32 [2, 4, 72, 64, 2048], P(None, None, None, 'lat', 'lon'), may hold values from 0 to 0.22
- vert_frac: float32 [2, 2, 72, 64, 2048], P(None, None, None, 'lat', 'lon'), may hold values from 0 to 0.4
- polar_shift: int32 [2, 4], replicated, may hold values from 1 to 4096
- polar_frac: float32 [2, 4], replicated, may hold values from 0 to 1
- sound_forcing: float32 [128, 128, 1152], P(('lat', 'lon')), may hold values from -6 to 6
- sound_col: int32 [128, 128, 16], P(('lat', 'lon')), may hold values from 0 to 1023
- sound_count: int32 [128, 128], P(('lat', 'lon')), may hold values from 0 to 16, as said below
Outputs:
- adjoint_out: float32 [16, 72, 64, 2048], P(None, None, 'lat', 'lon')
The draws below stay inside these ranges and needn't reach their ends.
Inputs may be any that keep to these rules, and one draw needn't show every extreme that they name: `sound_count`: in each draw some owning device has all 16 slots filled from every sender.
All inputs are finite; a program needn't handle non-finite values.
Results may differ from the reference program's by a relative error of at most 0.0003.
Values sent between devices are 32-bit elements; how exact they have to be, the bound alone decides.
A program may use at most 128 MiB of HBM per device.

```python
import jax
import jax.numpy as jnp
from jax import lax

TR = 16
LEV = 72
CLAT = 8
CLON = 128
NPOLE = 2
STEPS = 2
CAP = 16
NLAT = 64
NLON = 2048
NDEV = 128
N_LON = 16


def draw_sound_count(key, part):
    base = jax.random.fold_in(key, 7)
    first, second, third = jax.random.split(base, 3)
    level_owner = jax.random.randint(first, (NDEV, 1), CAP // 2, CAP + 1)
    dropped = jax.random.randint(second, (NDEV, NDEV), 0, CAP // 2 + 1)
    counts = jnp.maximum(level_owner - dropped, 0)
    busiest = jax.random.randint(third, (), 0, NDEV)
    owners = jnp.arange(NDEV)[:, None]
    counts = jnp.where(owners == busiest, CAP, counts)
    return counts.astype(jnp.int32)


def place_ends(array, own_key, least, largest):
    shape = array.shape
    spot = [jax.random.randint(jax.random.fold_in(own_key, axis), (), 0, shape[axis]) for axis in range(len(shape))]
    array = array.at[tuple(spot)].set(least)
    longest = shape.index(max(shape))
    spot[longest] = (spot[longest] + 1) % shape[longest]
    return array.at[tuple(spot)].set(largest)


def shard_levels(stream_key, extent, cuts, low, high):
    loudness, own = 1.0, jax.random.fold_in(stream_key, 6)
    for position, shards_of in cuts:
        steps = jnp.exp(jax.random.uniform(jax.random.fold_in(own, position), (shards_of,), jnp.float32, low / len(cuts), high / len(cuts)))
        loudness = loudness * jnp.repeat(steps, extent[position] // shards_of).reshape([-1 if axis == position else 1 for axis in range(len(extent))])
    return loudness


def bell_draw(own_key, extent, scale, reach, pieces=(), kind=jnp.bfloat16):
    entries = jax.random.normal(own_key, extent, jnp.float32) * scale
    if len(pieces) > 0:
        entries = shard_levels(own_key, extent, pieces, -0.22, 0.18) * entries
    return jnp.clip(entries, min=-reach, max=reach).astype(kind)


def setup_inputs(seed: int = 0) -> dict:
    key_of = jax.random.split(jax.random.key(seed), 9)
    adjoint_in = bell_draw(key_of[0], (TR, LEV, NLAT, NLON), 1.0, 6.0, ((2, 8), (3, 16)), jnp.float32)
    horiz_frac = jnp.clip(0.22 * jax.random.uniform(key_of[1], (STEPS, 4, LEV, NLAT, NLON), jnp.float32) ** shard_levels(key_of[1], (STEPS, 4, LEV, NLAT, NLON), ((3, 8), (4, 16)), -0.2, 0.2), 0.0, 0.22)
    vert_frac = jnp.clip(0.4 * jax.random.uniform(key_of[2], (STEPS, 2, LEV, NLAT, NLON), jnp.float32) ** shard_levels(key_of[2], (STEPS, 2, LEV, NLAT, NLON), ((3, 8), (4, 16)), -0.2, 0.2), 0.0, 0.4)
    polar_shift = place_ends(jax.random.randint(key_of[3], (STEPS, 2 * NPOLE), 1, 2 * NLON + 1), jax.random.fold_in(key_of[3], 1), 1, 2 * NLON).astype(jnp.int32)
    polar_frac = jnp.clip(jax.random.uniform(key_of[4], (STEPS, 2 * NPOLE), jnp.float32, 0.0, 1.0), 0.0, 1.0)
    sound_forcing = bell_draw(key_of[5], (NDEV, NDEV, CAP * LEV), 1.0, 6.0, ((0, 128),), jnp.float32)
    sound_col = place_ends(jax.random.randint(key_of[6], (NDEV, NDEV, CAP), 0, CLAT * CLON), jax.random.fold_in(key_of[6], 1), 0, (CLAT * CLON) - 1).astype(jnp.int32)
    sound_count = draw_sound_count(jax.random.fold_in(key_of[8], 71), 0)
    return dict(adjoint_in=adjoint_in, horiz_frac=horiz_frac, vert_frac=vert_frac, polar_shift=polar_shift, polar_frac=polar_frac, sound_forcing=sound_forcing, sound_col=sound_col, sound_count=sound_count)


def vertical(field, upward, downward):
    levels = field.shape[1]
    level_index = jnp.arange(levels)[:, None, None]
    upward = jnp.where(level_index < levels - 1, upward, 0.0)
    downward = jnp.where(level_index > 0, downward, 0.0)
    above_level = jnp.concatenate([field[:, 1:], field[:, -1:]], axis=1)
    below_level = jnp.concatenate([field[:, :1], field[:, :-1]], axis=1)
    return field + upward * (above_level - field) + downward * (below_level - field)


def polar_solve(field, shifts, fractions):
    polar_rows = jnp.concatenate([jnp.arange(NPOLE), jnp.arange(NLAT - NPOLE, NLAT)]).astype(jnp.int32)
    courant = shifts.astype(jnp.float32) + fractions
    retain = courant / (1.0 + courant)
    weight = 1.0 / (1.0 + courant)
    positions = jnp.arange(NLON, dtype=jnp.int32)
    distance = ((positions[:, None] - positions[None, :]) % NLON).astype(jnp.float32)
    selected = jnp.moveaxis(field[:, :, polar_rows, :], 2, 0)

    def solve_row(packed):
        row_data, row_retain, row_weight = packed
        log_retain = jnp.log(row_retain)
        matrix = jnp.exp(distance * log_retain) * (row_weight / (1.0 - jnp.exp(NLON * log_retain)))
        solved = jnp.dot(row_data.reshape(-1, NLON), matrix, precision=lax.Precision.HIGHEST)
        return solved.reshape(row_data.shape)

    solved = lax.map(solve_row, (selected, retain, weight))
    return field.at[:, :, polar_rows, :].set(jnp.moveaxis(solved, 0, 2))


def horizontal(field, fractions):
    global_row = jnp.arange(NLAT)[:, None]
    polar_mask = (global_row < NPOLE) | (global_row >= NLAT - NPOLE)
    eastward = jnp.where(polar_mask, 0.0, fractions[0])
    westward = jnp.where(polar_mask, 0.0, fractions[1])
    northward = jnp.where(global_row == NLAT - 1, 0.0, fractions[2])
    southward = jnp.where(global_row == 0, 0.0, fractions[3])
    east_cell = jnp.roll(field, -1, axis=3)
    west_cell = jnp.roll(field, 1, axis=3)
    north_cell = jnp.roll(field, -1, axis=2)
    south_cell = jnp.roll(field, 1, axis=2)
    return (field + eastward * (east_cell - field) + westward * (west_cell - field)
            + northward * (north_cell - field) + southward * (south_cell - field))


def reference(adjoint_in, horiz_frac, vert_frac, polar_shift, polar_frac, sound_forcing, sound_col, sound_count):
    device = jnp.arange(NDEV, dtype=jnp.int32)
    lat_index = device // N_LON
    lon_index = device % N_LON
    global_row = lat_index[:, None, None] * CLAT + sound_col // CLON
    global_col = lon_index[:, None, None] * CLON + sound_col % CLON
    flat_index = (global_row * NLON + global_col).reshape(-1).astype(jnp.int32)
    values = jnp.transpose(sound_forcing.reshape(NDEV, NDEV, CAP, LEV), (1, 0, 2, 3))
    filled = jnp.arange(CAP, dtype=jnp.int32)[None, None, :] < sound_count[:, :, None]
    values = jnp.where(filled[..., None], values, 0.0)
    forcing = jnp.zeros((LEV, NLAT * NLON), jnp.float32).at[:, flat_index].add(values.reshape(-1, LEV).T)
    field = adjoint_in + forcing.reshape(LEV, NLAT, NLON)[None]
    for step_index in range(STEPS - 1, -1, -1):
        mixed = vertical(field, vert_frac[step_index, 0], vert_frac[step_index, 1])
        polar = polar_solve(mixed, polar_shift[step_index], polar_frac[step_index])
        field = horizontal(polar, horiz_frac[step_index])
    return field
```

```python
import functools

import jax
import jax.numpy as jnp
from jax import lax
from jax.experimental import pallas as pl
from jax.experimental.pallas import tpu as pltpu
from jax.sharding import PartitionSpec as P

MESH = pl.DeviceIdType.MESH
NPOLE = 2
STEPS = 2
GROUP = 4
PITCH = 16
BLOCK = 8
HIGH = lax.Precision.HIGHEST


def log_of(value):
    shifted = value - 1.0
    z = shifted / (2.0 + shifted)
    square = z * z
    total = jnp.full_like(z, 1.0 / 17.0)
    for odd in (15, 13, 11, 9, 7, 5, 3, 1):
        total = total * square + 1.0 / odd
    return 2.0 * z * total


def kernel(
    sizes,
    shift_ref,
    frac_ref,
    adjoint_hbm,
    horiz_hbm,
    vert_hbm,
    value_hbm,
    col_ref,
    count_ref,
    out_hbm,
    field,
    horiz,
    vert,
    value,
    padded,
    forcing,
    mixed_forcing,
    owned,
    parts,
    turned,
    row_send,
    row_recv,
    col_send,
    col_recv,
    pole_send,
    pole_recv,
    pole_matrix,
    load_sem,
    out_sem,
    row_send_sem,
    row_recv_sem,
    col_send_sem,
    col_recv_sem,
    pole_send_sem,
    pole_recv_sem,
):
    tracers, levels, lats, lons, n_lat, n_lon, slots = sizes
    groups = tracers // GROUP
    blocks = levels // BLOCK
    per_group = GROUP * levels
    lat = lax.axis_index("lat")
    lon = lax.axis_index("lon")
    north = lax.rem(lat + 1, n_lat)
    south = lax.rem(lat + n_lat - 1, n_lat)
    east = lax.rem(lon + 1, n_lon)
    west = lax.rem(lon + n_lon - 1, n_lon)
    at_top = lat == 0
    is_polar = at_top | (lat == n_lat - 1)
    pole_row = jnp.where(at_top, 0, lats - NPOLE)
    first_pole = jnp.where(at_top, 0, NPOLE)

    lane = lax.broadcasted_iota(jnp.int32, (lats, lons), 1)
    sub = lax.broadcasted_iota(jnp.int32, (lats, lons), 0)

    loads = [
        pltpu.make_async_copy(value_hbm, value, load_sem.at[0]),
        pltpu.make_async_copy(vert_hbm, vert, load_sem.at[1]),
        pltpu.make_async_copy(adjoint_hbm, field, load_sem.at[2]),
        pltpu.make_async_copy(horiz_hbm, horiz, load_sem.at[3]),
    ]
    for copy in loads:
        copy.start()

    barrier = pltpu.get_barrier_semaphore()
    for target in ((north, lon), (south, lon), (lat, east), (lat, west)):
        pl.semaphore_signal(barrier, inc=1, device_id=target, device_id_type=MESH)

    @pl.when(is_polar)
    def _():
        for d in range(1, n_lon):
            pl.semaphore_signal(
                barrier, inc=1, device_id=(lat, lax.rem(lon + d, n_lon)), device_id_type=MESH
            )

    pl.semaphore_wait(barrier, jnp.where(is_polar, n_lon + 3, 4))

    def courant(step, p):
        return shift_ref[step, first_pole + p].astype(jnp.float32) + frac_ref[step, first_pole + p]

    def log_retain(step, p, shape):
        c = jnp.full(shape, courant(step, p), jnp.float32)
        return log_of(c / (1.0 + c))

    @pl.when(is_polar)
    def _():
        j = lax.broadcasted_iota(jnp.int32, (lons, lons), 0)
        i = lax.broadcasted_iota(jnp.int32, (lons, lons), 1)
        distance = (j - i).astype(jnp.float32)
        for step in range(STEPS):
            for p in range(NPOLE):
                power = jnp.exp(
                    jnp.maximum(distance, 0.0) * log_retain(step, p, (lons, lons))
                )
                weight = 1.0 / (1.0 + jnp.full((lons, lons), courant(step, p), jnp.float32))
                pole_matrix[step, p] = jnp.where(distance >= 0.0, power, 0.0) * weight

    senders = value.shape[0]
    counts = jnp.broadcast_to(count_ref[...], (senders, senders)).T
    slot = lax.broadcasted_iota(jnp.int32, (senders, slots), 1)
    columns = jnp.where(slot < counts[:, :slots], col_ref[...], -1)
    for j in range(slots):
        owned[j * senders : (j + 1) * senders, :] = jnp.broadcast_to(
            columns[:, j : j + 1], (senders, lons)
        )
    loads[0].wait()
    for i in range(value.shape[1] // lons):
        turned[i * lons : (i + 1) * lons, :] = value[:, i * lons : (i + 1) * lons].T
    gap = jnp.zeros((8, senders), jnp.float32)
    for j in range(slots):
        piece = turned[j * levels : (j + 1) * levels, :]
        high = piece.astype(jnp.bfloat16).astype(jnp.float32)
        rest = piece - high
        middle = rest.astype(jnp.bfloat16).astype(jnp.float32)
        low = rest - middle
        stacked = jnp.concatenate([high, gap, middle, gap, low, gap], axis=0)
        parts[:, j * senders : (j + 1) * senders] = stacked.astype(jnp.bfloat16)

    span = levels + 8

    def place(pair, carry):
        here = lax.broadcasted_iota(jnp.int32, (slots * senders, lons), 1) + pair * (2 * lons)
        cols = owned[...]
        hot = jnp.concatenate(
            [
                jnp.where(cols == here, 1.0, 0.0).astype(jnp.bfloat16),
                jnp.where(cols == here + lons, 1.0, 0.0).astype(jnp.bfloat16),
            ],
            axis=1,
        )
        got = jnp.dot(parts[...], hot, preferred_element_type=jnp.float32)
        total = got[:levels] + got[span : span + levels] + got[2 * span : 2 * span + levels]
        forcing[pl.ds(2 * pair, levels, stride=lats), :] = total[:, :lons]
        forcing[pl.ds(2 * pair + 1, levels, stride=lats), :] = total[:, lons:]
        return carry

    lax.fori_loop(0, lats // 2, place, 0)
    loads[1].wait()

    def mix_forcing(level, carry):
        up = vert[STEPS - 1, 0, level]
        down = vert[STEPS - 1, 1, level]
        start = pl.multiple_of(level * lats, lats)
        above = pl.multiple_of(jnp.minimum(level + 1, levels - 1) * lats, lats)
        below = pl.multiple_of(jnp.maximum(level - 1, 0) * lats, lats)
        here = forcing[pl.ds(start, lats), :]
        mixed_forcing[level] = (
            (1.0 - up - down) * here
            + up * forcing[pl.ds(above, lats), :]
            + down * forcing[pl.ds(below, lats), :]
        )
        return carry

    lax.fori_loop(0, levels, mix_forcing, 0)
    loads[2].wait()

    pair_index = ((lane + 1) >> 1) & (lons // 2 - 1)

    def tile_base(t, level):
        return (t * levels + level) * PITCH + 8

    def vertical(g, step):
        def block(lb, carry):
            first = lb * BLOCK
            before = jnp.maximum(first - 1, 0)
            down_tiles = [field[g * GROUP + t, before] for t in range(GROUP)]
            here_tiles = [field[g * GROUP + t, first] for t in range(GROUP)]
            packed = jnp.zeros((lats, lons), jnp.float32)
            for dl in range(BLOCK):
                level = first + dl
                after = jnp.minimum(level + 1, levels - 1)
                up = vert[step, 0, level]
                down = vert[step, 1, level]
                keep = 1.0 - up - down
                for t in range(GROUP):
                    up_tile = field[g * GROUP + t, after]
                    mixed = keep * here_tiles[t] + up * up_tile + down * down_tiles[t]
                    if step == STEPS - 1:
                        mixed = mixed + mixed_forcing[level]
                    start = pl.multiple_of(tile_base(g * GROUP + t, level), 8)
                    padded[pl.ds(start, lats), :] = mixed
                    k = dl * GROUP + t
                    turn = mixed if k == 0 else pltpu.roll(mixed, 2 * k, 1)
                    packed = jnp.where(pair_index == k, turn, packed)
                    down_tiles[t] = here_tiles[t]
                    here_tiles[t] = up_tile
            col_send[step, g, lb] = packed
            for t in range(GROUP):
                start = tile_base(g * GROUP + t, first)
                to = pl.multiple_of(t * levels + first, 8)
                row_send[step, 0, g, pl.ds(to, BLOCK), :] = padded[
                    pl.ds(start, BLOCK, stride=PITCH), :
                ]
                row_send[step, 1, g, pl.ds(to, BLOCK), :] = padded[
                    pl.ds(start + lats - 1, BLOCK, stride=PITCH), :
                ]
            return carry

        lax.fori_loop(0, blocks, block, 0)

    def row_copy(g, step, side):
        target = (south, lon) if side == 0 else (north, lon)
        return pltpu.make_async_remote_copy(
            src_ref=row_send.at[step, side, g],
            dst_ref=row_recv.at[step, side, g],
            send_sem=row_send_sem.at[step, side, g],
            recv_sem=row_recv_sem.at[step, side, g],
            device_id=target,
            device_id_type=MESH,
        )

    def col_copy(g, step, side):
        target = (lat, west) if side == 0 else (lat, east)
        return pltpu.make_async_remote_copy(
            src_ref=col_send.at[step, g],
            dst_ref=col_recv.at[step, side, g],
            send_sem=col_send_sem.at[step, side, g],
            recv_sem=col_recv_sem.at[step, side, g],
            device_id=target,
            device_id_type=MESH,
        )

    def pole_copy(g, step, d):
        return pltpu.make_async_remote_copy(
            src_ref=pole_send.at[step, g],
            dst_ref=pole_recv.at[step, g, n_lon - d],
            send_sem=pole_send_sem.at[step, g, d],
            recv_sem=pole_recv_sem.at[step, g, n_lon - d],
            device_id=(lat, lax.rem(lon + d, n_lon)),
            device_id_type=MESH,
        )

    def pole_local(g, step):
        @pl.when(is_polar)
        def _():
            packed = jnp.zeros((lats, lons), jnp.float32)
            for p in range(NPOLE):
                for t in range(GROUP):
                    start = tile_base(g * GROUP + t, 0) + pole_row + p
                    rows = padded[pl.ds(start, levels, stride=PITCH), :]
                    solved = jnp.dot(
                        rows,
                        pole_matrix[step, p],
                        precision=HIGH,
                        preferred_element_type=jnp.float32,
                    )
                    padded[pl.ds(start, levels, stride=PITCH), :] = solved
                    for lb in range(blocks):
                        q = (p * GROUP + t) * blocks + lb
                        tile = solved[lb * 8 : lb * 8 + 8]
                        turn = tile if q == 0 else pltpu.roll(tile, q, 1)
                        packed = jnp.where(lane == q, turn, packed)
            pole_send[step, g] = packed
            for d in range(1, n_lon):
                pole_copy(g, step, d).start()

    def pole_finish(g, step):
        @pl.when(is_polar)
        def _():
            for d in range(1, n_lon):
                pole_copy(g, step, d).wait_recv()
            logs = [log_retain(step, p, (lats, lons)) for p in range(NPOLE)]
            log = jnp.where(lane < GROUP * blocks, logs[0], logs[1])
            inflow = pole_send[step, g] * jnp.exp((float(lons) * (n_lon - 1)) * log)
            for d in range(1, n_lon):
                inflow = inflow + pole_recv[step, g, d] * jnp.exp((float(lons) * (d - 1)) * log)
            inflow = inflow / (1.0 - jnp.exp(float(lons * n_lon) * log))
            for p in range(NPOLE):
                carried = jnp.exp((lons - lane).astype(jnp.float32) * logs[p])
                for t in range(GROUP):
                    for lb in range(blocks):
                        q = (p * GROUP + t) * blocks + lb
                        start = tile_base(g * GROUP + t, lb * BLOCK) + pole_row + p
                        spread = jnp.broadcast_to(inflow[:, q : q + 1], (lats, lons))
                        padded[pl.ds(start, BLOCK, stride=PITCH), :] = (
                            padded[pl.ds(start, BLOCK, stride=PITCH), :] + carried * spread
                        )

    global_row = lat * lats + sub
    polar_mask = (global_row < NPOLE) | (global_row >= n_lat * lats - NPOLE)
    zero = jnp.zeros((lats, lons), jnp.float32)

    def horizontal(g, step):
        def block(lb, carry):
            first = lb * BLOCK
            halo = jnp.where(
                (lane & 1) == 0,
                col_recv[step, 0, g, lb],
                pltpu.roll(col_recv[step, 1, g, lb], 2, 1),
            )
            for t in range(GROUP):
                start = tile_base(g * GROUP + t, first)
                at = pl.multiple_of(t * levels + first, 8)
                padded[pl.ds(start + lats, BLOCK, stride=PITCH), :] = row_recv[
                    step, 0, g, pl.ds(at, BLOCK), :
                ]
                padded[pl.ds(start - 1, BLOCK, stride=PITCH), :] = row_recv[
                    step, 1, g, pl.ds(at, BLOCK), :
                ]
            for dl in range(BLOCK):
                level = first + dl
                e = jnp.where(polar_mask, zero, horiz[step, 0, level])
                w = jnp.where(polar_mask, zero, horiz[step, 1, level])
                n = jnp.where(global_row == n_lat * lats - 1, zero, horiz[step, 2, level])
                s = jnp.where(global_row == 0, zero, horiz[step, 3, level])
                keep = 1.0 - e - w - n - s
                edge = jnp.where(lane == lons - 1, e, jnp.where(lane == 0, w, zero))
                e = jnp.where(lane == lons - 1, zero, e)
                w = jnp.where(lane == 0, zero, w)
                for t in range(GROUP):
                    start = pl.multiple_of(tile_base(g * GROUP + t, level), 8)
                    here = padded[pl.ds(start, lats), :]
                    k = dl * GROUP + t
                    field[g * GROUP + t, level] = (
                        keep * here
                        + e * pltpu.roll(here, lons - 1, 1)
                        + w * pltpu.roll(here, 1, 1)
                        + edge * pltpu.roll(halo, lons - 1 - 2 * k, 1)
                        + n * padded[pl.ds(start + 1, lats), :]
                        + s * padded[pl.ds(start - 1, lats), :]
                    )
            return carry

        lax.fori_loop(0, blocks, block, 0)

    def release(g, step):
        for side in range(2):
            row_copy(g, step, side).start()
            col_copy(g, step, side).start()

    def receive(g, step):
        for side in range(2):
            row_copy(g, step, side).wait_recv()
            col_copy(g, step, side).wait_recv()

    def first_phase(g, carry):
        vertical(g, STEPS - 1)
        release(g, STEPS - 1)
        pole_local(g, STEPS - 1)
        return carry

    lax.fori_loop(0, groups, first_phase, 0)
    loads[3].wait()

    for step in range(STEPS - 1, 0, -1):

        def middle_phase(g, carry):
            receive(g, step)
            pole_finish(g, step)
            horizontal(g, step)
            vertical(g, step - 1)
            release(g, step - 1)
            pole_local(g, step - 1)
            return carry

        lax.fori_loop(0, groups, middle_phase, 0)

    def out_copy(g):
        return pltpu.make_async_copy(
            field.at[pl.ds(g * GROUP, GROUP)], out_hbm.at[pl.ds(g * GROUP, GROUP)], out_sem.at[g]
        )

    def last_phase(g, carry):
        receive(g, 0)
        pole_finish(g, 0)
        horizontal(g, 0)
        out_copy(g).start()
        return carry

    lax.fori_loop(0, groups, last_phase, 0)

    def drain(g, carry):
        out_copy(g).wait()
        for step in range(STEPS):
            for side in range(2):
                row_copy(g, step, side).wait_send()
                col_copy(g, step, side).wait_send()

            @pl.when(is_polar)
            def _():
                for d in range(1, n_lon):
                    pole_copy(g, step, d).wait_send()

        return carry

    lax.fori_loop(0, groups, drain, 0)


def transport(mesh_shape, adjoint_in, horiz_frac, vert_frac, shift, frac, values, cols, counts):
    tracers, levels, lats, lons = adjoint_in.shape
    n_lat, n_lon = mesh_shape
    senders, slots = cols.shape
    groups = tracers // GROUP
    blocks = levels // BLOCK
    per_group = GROUP * levels
    f32 = jnp.float32
    any_spec = pl.BlockSpec(memory_space=pl.ANY)
    vmem = pl.BlockSpec(memory_space=pltpu.VMEM)
    smem = pl.BlockSpec(memory_space=pltpu.SMEM)
    dma = pltpu.SemaphoreType.DMA
    return pl.pallas_call(
        functools.partial(kernel, (tracers, levels, lats, lons, n_lat, n_lon, slots)),
        out_shape=jax.ShapeDtypeStruct(adjoint_in.shape, f32),
        in_specs=[smem, smem, any_spec, any_spec, any_spec, any_spec, vmem, vmem],
        out_specs=any_spec,
        scratch_shapes=[
            pltpu.VMEM(adjoint_in.shape, f32),
            pltpu.VMEM(horiz_frac.shape, f32),
            pltpu.VMEM(vert_frac.shape, f32),
            pltpu.VMEM(values.shape, f32),
            pltpu.VMEM((tracers * levels * PITCH + 32, lons), f32),
            pltpu.VMEM((levels * lats, lons), f32),
            pltpu.VMEM((levels, lats, lons), f32),
            pltpu.VMEM((slots * senders, lons), jnp.int32),
            pltpu.VMEM((3 * (levels + 8), slots * senders), jnp.bfloat16),
            pltpu.VMEM((values.shape[1], senders), f32),
            pltpu.VMEM((STEPS, 2, groups, per_group, lons), f32),
            pltpu.VMEM((STEPS, 2, groups, per_group, lons), f32),
            pltpu.VMEM((STEPS, groups, blocks, lats, lons), f32),
            pltpu.VMEM((STEPS, 2, groups, blocks, lats, lons), f32),
            pltpu.VMEM((STEPS, groups, lats, lons), f32),
            pltpu.VMEM((STEPS, groups, n_lon, lats, lons), f32),
            pltpu.VMEM((STEPS, NPOLE, lons, lons), f32),
            dma((4,)),
            dma((groups,)),
            dma((STEPS, 2, groups)),
            dma((STEPS, 2, groups)),
            dma((STEPS, 2, groups)),
            dma((STEPS, 2, groups)),
            dma((STEPS, groups, n_lon)),
            dma((STEPS, groups, n_lon)),
        ],
        compiler_params=pltpu.CompilerParams(
            collective_id=0, has_side_effects=True, vmem_limit_bytes=60 * 1024 * 1024
        ),
    )(shift, frac, adjoint_in, horiz_frac, vert_frac, values, cols, counts)


def solution(mesh):
    mesh_shape = (mesh.shape["lat"], mesh.shape["lon"])

    def on_device(
        adjoint_in,
        horiz_frac,
        vert_frac,
        polar_shift,
        polar_frac,
        sound_forcing,
        sound_col,
        sound_count,
    ):
        received = lax.all_to_all(
            sound_forcing, ("lat", "lon"), split_axis=1, concat_axis=0, tiled=True
        )
        values = received.reshape(received.shape[0], received.shape[2])
        return transport(
            mesh_shape,
            adjoint_in,
            horiz_frac,
            vert_frac,
            polar_shift,
            polar_frac,
            values,
            sound_col[0],
            sound_count,
        )

    return jax.shard_map(
        on_device,
        mesh=mesh,
        in_specs=(
            P(None, None, "lat", "lon"),
            P(None, None, None, "lat", "lon"),
            P(None, None, None, "lat", "lon"),
            P(),
            P(),
            P(("lat", "lon"), None, None),
            P(("lat", "lon"), None, None),
            P(("lat", "lon"), None),
        ),
        out_specs=P(None, None, "lat", "lon"),
        check_vma=False,
    )
```

```python
import functools

import jax
import jax.numpy as jnp
from jax import lax
from jax.experimental import pallas as pl
from jax.experimental.pallas import tpu as pltpu
from jax.sharding import PartitionSpec as P

MESH = pl.DeviceIdType.MESH
NPOLE = 2
STEPS = 2
GROUP = 4
PITCH = 16
BLOCK = 8


def log_of(value):
    shifted = value - 1.0
    z = shifted / (2.0 + shifted)
    square = z * z
    total = jnp.full_like(z, 1.0 / 17.0)
    for odd in (15, 13, 11, 9, 7, 5, 3, 1):
        total = total * square + 1.0 / odd
    return 2.0 * z * total


def halves(value):
    high = value.astype(jnp.bfloat16)
    return high, (value - high.astype(jnp.float32)).astype(jnp.bfloat16)


def kernel(
    sizes,
    shift_ref,
    frac_ref,
    adjoint_hbm,
    horiz_hbm,
    vert_hbm,
    sound_hbm,
    col_ref,
    count_ref,
    out_hbm,
    extra_hbm,
    field,
    horiz,
    vert,
    padded,
    owned,
    parts,
    turned,
    first_recv,
    second_send,
    second_recv,
    row_send,
    row_recv,
    col_send,
    col_recv,
    pole_send,
    pole_recv,
    pole_part,
    extra_row_send,
    extra_row_recv,
    extra_col_send,
    extra_col_recv,
    extra_pole_send,
    extra_pole_recv,
    extra_pole_part,
    pole_matrix,
    load_sem,
    out_sem,
    first_send_sem,
    first_recv_sem,
    second_send_sem,
    second_recv_sem,
    row_send_sem,
    row_recv_sem,
    col_send_sem,
    col_recv_sem,
    pole_send_sem,
    pole_recv_sem,
):
    tracers, levels, lats, lons, n_lat, n_lon, slots = sizes
    groups = tracers // GROUP
    blocks = levels // BLOCK
    senders = n_lat * n_lon
    chunks = slots * levels // lons
    lat = lax.axis_index("lat")
    lon = lax.axis_index("lon")
    north = lax.rem(lat + 1, n_lat)
    south = lax.rem(lat + n_lat - 1, n_lat)
    east = lax.rem(lon + 1, n_lon)
    west = lax.rem(lon + n_lon - 1, n_lon)
    at_top = lat == 0
    is_polar = at_top | (lat == n_lat - 1)
    pole_row = jnp.where(at_top, 0, lats - NPOLE)
    first_pole = jnp.where(at_top, 0, NPOLE)

    lane = lax.broadcasted_iota(jnp.int32, (lats, lons), 1)
    sub = lax.broadcasted_iota(jnp.int32, (lats, lons), 0)

    volume = tracers * levels * lats
    load_vert = pltpu.make_async_copy(vert_hbm, vert, load_sem.at[0])
    load_field = pltpu.make_async_copy(adjoint_hbm, field.at[pl.ds(0, volume)], load_sem.at[1])
    load_horiz = pltpu.make_async_copy(horiz_hbm, horiz, load_sem.at[2])
    load_own = pltpu.make_async_copy(
        sound_hbm.at[pl.ds(lat * n_lon, n_lon)], first_recv.at[lat], load_sem.at[3]
    )
    load_vert.start()
    load_field.start()
    load_horiz.start()
    load_own.start()

    barrier = pltpu.get_barrier_semaphore()
    for d in range(1, n_lat):
        pl.semaphore_signal(
            barrier, inc=1, device_id=(lax.rem(lat + d, n_lat), lon), device_id_type=MESH
        )
    for d in range(1, n_lon):
        pl.semaphore_signal(
            barrier, inc=1, device_id=(lat, lax.rem(lon + d, n_lon)), device_id_type=MESH
        )

    def courant(step, p):
        return shift_ref[step, first_pole + p].astype(jnp.float32) + frac_ref[step, first_pole + p]

    def log_retain(step, p, shape):
        c = jnp.full(shape, courant(step, p), jnp.float32)
        return log_of(c / (1.0 + c))

    @pl.when(is_polar)
    def _():
        j = lax.broadcasted_iota(jnp.int32, (lons, lons), 0)
        i = lax.broadcasted_iota(jnp.int32, (lons, lons), 1)
        distance = (j - i).astype(jnp.float32)
        for step in range(STEPS):
            for p in range(NPOLE):
                power = jnp.exp(jnp.maximum(distance, 0.0) * log_retain(step, p, (lons, lons)))
                weight = 1.0 / (1.0 + jnp.full((lons, lons), courant(step, p), jnp.float32))
                matrix = jnp.where(distance >= 0.0, power, 0.0) * weight
                high, low = halves(matrix)
                pole_matrix[step, p, 0:lons, :] = high
                pole_matrix[step, p, lons : 2 * lons, :] = high
                pole_matrix[step, p, 2 * lons : 3 * lons, :] = low

    counts = jnp.broadcast_to(count_ref[...], (senders, senders)).T
    slot = lax.broadcasted_iota(jnp.int32, (senders, slots), 1)
    columns = jnp.where(slot < counts[:, :slots], col_ref[...], -1)
    for j in range(slots):
        spread = jnp.broadcast_to(columns[:, j : j + 1], (senders, lons))
        for a in range(n_lat):
            owned[pl.ds(j * senders + a, n_lon, stride=n_lat), :] = spread[
                a * n_lon : (a + 1) * n_lon
            ]

    pl.semaphore_wait(barrier, n_lat + n_lon - 2)

    def first_copy(d):
        target = lax.rem(lat + d, n_lat)
        return pltpu.make_async_remote_copy(
            src_ref=sound_hbm.at[pl.ds(target * n_lon, n_lon)],
            dst_ref=first_recv.at[lat],
            send_sem=first_send_sem.at[d],
            recv_sem=first_recv_sem.at[lat],
            device_id=(target, lon),
            device_id_type=MESH,
        )

    def first_arrival(d):
        source = lax.rem(lat + d, n_lat)
        return pltpu.make_async_remote_copy(
            src_ref=first_recv.at[source],
            dst_ref=first_recv.at[source],
            send_sem=first_send_sem.at[d],
            recv_sem=first_recv_sem.at[source],
            device_id=(source, lon),
            device_id_type=MESH,
        )

    share = chunks * n_lat

    def second_copy(d):
        target = lax.rem(lon + d, n_lon)
        return pltpu.make_async_remote_copy(
            src_ref=second_send.at[pl.ds(target * share, share)],
            dst_ref=second_recv.at[pl.ds(lon * share, share)],
            send_sem=second_send_sem.at[d],
            recv_sem=second_recv_sem.at[lon],
            device_id=(lat, target),
            device_id_type=MESH,
        )

    def second_arrival(d):
        source = lax.rem(lon + d, n_lon)
        here = second_recv.at[pl.ds(source * share, share)]
        return pltpu.make_async_remote_copy(
            src_ref=here,
            dst_ref=here,
            send_sem=second_send_sem.at[d],
            recv_sem=second_recv_sem.at[source],
            device_id=(lat, source),
            device_id_type=MESH,
        )

    second_own = pltpu.make_async_copy(
        second_send.at[pl.ds(lon * share, share)],
        second_recv.at[pl.ds(lon * share, share)],
        second_recv_sem.at[lon],
    )

    for d in range(1, n_lat):
        first_copy(d).start()

    def forward():
        load_own.wait()
        for d in range(1, n_lat):
            first_arrival(d).wait_recv()
        for a in range(n_lat):
            for half in range(n_lon // 8):
                for i in range(chunks):
                    second_send[pl.ds((half * 8 * chunks + i) * n_lat + a, 8, stride=share), :] = (
                        first_recv[a, half * 8 : half * 8 + 8, i * lons : (i + 1) * lons]
                    )
        for d in range(1, n_lon):
            second_copy(d).start()
        second_own.start()

    extra_base = tracers * levels * lats

    def collect():
        second_own.wait()
        for d in range(1, n_lon):
            second_arrival(d).wait_recv()
        for i in range(chunks):
            rows = [
                second_recv[(b * chunks + i) * n_lat : (b * chunks + i + 1) * n_lat, :]
                for b in range(n_lon)
            ]
            turned[i * lons : (i + 1) * lons, :] = jnp.concatenate(rows, axis=0).T
        gap = jnp.zeros((8, senders), jnp.float32)
        for j in range(slots):
            piece = turned[j * levels : (j + 1) * levels, :]
            high = piece.astype(jnp.bfloat16).astype(jnp.float32)
            rest = piece - high
            middle = rest.astype(jnp.bfloat16).astype(jnp.float32)
            low = rest - middle
            stacked = jnp.concatenate([high, gap, middle, gap, low, gap], axis=0)
            parts[:, j * senders : (j + 1) * senders] = stacked.astype(jnp.bfloat16)
        span = levels + 8

        def place(pair, carry):
            here = lax.broadcasted_iota(jnp.int32, (slots * senders, lons), 1) + pair * (2 * lons)
            cols = owned[...]
            hot = jnp.concatenate(
                [
                    jnp.where(cols == here, 1.0, 0.0).astype(jnp.bfloat16),
                    jnp.where(cols == here + lons, 1.0, 0.0).astype(jnp.bfloat16),
                ],
                axis=1,
            )
            got = jnp.dot(parts[...], hot, preferred_element_type=jnp.float32)
            total = got[:levels] + got[span : span + levels] + got[2 * span : 2 * span + levels]
            field[pl.ds(extra_base + 2 * pair, levels, stride=lats), :] = total[:, :lons]
            field[pl.ds(extra_base + 2 * pair + 1, levels, stride=lats), :] = total[:, lons:]
            return carry

        lax.fori_loop(0, lats // 2, place, 0)

    pair_index = ((lane + 1) >> 1) & (lons // 2 - 1)
    global_row = lat * lats + sub
    polar_mask = (global_row < NPOLE) | (global_row >= n_lat * lats - NPOLE)
    zero = jnp.zeros((lats, lons), jnp.float32)

    class Part:
        def __init__(self, first, count, index, buffers):
            self.first, self.count, self.index = first, count, index
            self.extra = index == groups if isinstance(index, int) else False
            (
                self.row_send,
                self.row_recv,
                self.col_send,
                self.col_recv,
                self.pole_send,
                self.pole_recv,
                self.pole_part,
            ) = buffers

        def base(self, t, level):
            return ((self.first + t) * levels + level) * PITCH + 8

        def tile(self, t, level):
            return pl.ds(pl.multiple_of(((self.first + t) * levels + level) * lats, lats), lats)

        def vertical(self, step):
            count = self.count

            def block(lb, carry):
                first = lb * BLOCK
                before = jnp.maximum(first - 1, 0)
                down_tiles = [field[self.tile(t, before), :] for t in range(count)]
                here_tiles = [field[self.tile(t, first), :] for t in range(count)]
                packed = zero
                for dl in range(BLOCK):
                    level = first + dl
                    after = jnp.minimum(level + 1, levels - 1)
                    up = vert[step, 0, level]
                    down = vert[step, 1, level]
                    keep = 1.0 - up - down
                    for t in range(count):
                        up_tile = field[self.tile(t, after), :]
                        mixed = keep * here_tiles[t] + up * up_tile + down * down_tiles[t]
                        start = pl.multiple_of(self.base(t, level), 8)
                        padded[pl.ds(start, lats), :] = mixed
                        k = dl * count + t
                        turn = mixed if k == 0 else pltpu.roll(mixed, 2 * k, 1)
                        packed = jnp.where(pair_index == k, turn, packed)
                        down_tiles[t] = here_tiles[t]
                        here_tiles[t] = up_tile
                self.col_send(step)[lb] = packed
                for t in range(count):
                    start = self.base(t, first)
                    to = pl.multiple_of(t * levels + first, 8)
                    self.row_send(step, 0)[pl.ds(to, BLOCK), :] = padded[
                        pl.ds(start, BLOCK, stride=PITCH), :
                    ]
                    self.row_send(step, 1)[pl.ds(to, BLOCK), :] = padded[
                        pl.ds(start + lats - 1, BLOCK, stride=PITCH), :
                    ]
                return carry

            lax.fori_loop(0, blocks, block, 0)

        def row_copy(self, step, side):
            return pltpu.make_async_remote_copy(
                src_ref=self.row_send(step, side),
                dst_ref=self.row_recv(step, side),
                send_sem=row_send_sem.at[step, side, self.index],
                recv_sem=row_recv_sem.at[step, side, self.index],
                device_id=(south, lon) if side == 0 else (north, lon),
                device_id_type=MESH,
            )

        def col_copy(self, step, side):
            return pltpu.make_async_remote_copy(
                src_ref=self.col_send(step),
                dst_ref=self.col_recv(step, side),
                send_sem=col_send_sem.at[step, side, self.index],
                recv_sem=col_recv_sem.at[step, side, self.index],
                device_id=(lat, west) if side == 0 else (lat, east),
                device_id_type=MESH,
            )

        def pole_copy(self, step, d):
            return pltpu.make_async_remote_copy(
                src_ref=self.pole_send(step),
                dst_ref=self.pole_recv(step).at[n_lon - d],
                send_sem=pole_send_sem.at[step, self.index, d],
                recv_sem=pole_recv_sem.at[step, self.index, n_lon - d],
                device_id=(lat, lax.rem(lon + d, n_lon)),
                device_id_type=MESH,
            )

        def release(self, step):
            for side in range(2):
                self.row_copy(step, side).start()
                self.col_copy(step, side).start()

        def receive(self, step):
            for side in range(2):
                self.row_copy(step, side).wait_recv()
                self.col_copy(step, side).wait_recv()

        def pole_local(self, step):
            count = self.count

            @pl.when(is_polar)
            def _():
                packed = zero
                for p in range(NPOLE):
                    start = self.base(0, 0) + pole_row + p
                    rows = padded[pl.ds(start, count * levels, stride=PITCH), :]
                    high, low = halves(rows)
                    solved = jnp.dot(
                        jnp.concatenate([high, low, high], axis=1),
                        pole_matrix[step, p],
                        preferred_element_type=jnp.float32,
                    )
                    self.pole_part(step)[p] = solved
                    for q in range(count * blocks):
                        tile = solved[q * 8 : q * 8 + 8]
                        at = p * count * blocks + q
                        turn = tile if at == 0 else pltpu.roll(tile, at, 1)
                        packed = jnp.where(lane == at, turn, packed)
                self.pole_send(step)[...] = packed
                for d in range(1, n_lon):
                    self.pole_copy(step, d).start()

        def pole_finish(self, step):
            count = self.count

            @pl.when(is_polar)
            def _():
                for d in range(1, n_lon):
                    self.pole_copy(step, d).wait_recv()
                logs = [log_retain(step, p, (lats, lons)) for p in range(NPOLE)]
                log = jnp.where(lane < count * blocks, logs[0], logs[1])
                inflow = self.pole_send(step)[...] * jnp.exp((float(lons) * (n_lon - 1)) * log)
                for d in range(1, n_lon):
                    inflow = inflow + self.pole_recv(step)[d] * jnp.exp(
                        (float(lons) * (d - 1)) * log
                    )
                inflow = inflow / (1.0 - jnp.exp(float(lons * n_lon) * log))
                for p in range(NPOLE):
                    carried = jnp.exp((lons - lane).astype(jnp.float32) * logs[p])
                    for q in range(count * blocks):
                        at = p * count * blocks + q
                        start = self.base(0, q * BLOCK) + pole_row + p
                        spread = jnp.broadcast_to(inflow[:, at : at + 1], (lats, lons))
                        padded[pl.ds(start, BLOCK, stride=PITCH), :] = (
                            self.pole_part(step)[p, q * 8 : q * 8 + 8, :] + carried * spread
                        )

        def horizontal(self, step):
            count = self.count

            def block(lb, carry):
                first = lb * BLOCK
                halo = jnp.where(
                    (lane & 1) == 0,
                    self.col_recv(step, 0)[lb],
                    pltpu.roll(self.col_recv(step, 1)[lb], 2, 1),
                )
                for t in range(count):
                    start = self.base(t, first)
                    at = pl.multiple_of(t * levels + first, 8)
                    padded[pl.ds(start + lats, BLOCK, stride=PITCH), :] = self.row_recv(step, 0)[
                        pl.ds(at, BLOCK), :
                    ]
                    padded[pl.ds(start - 1, BLOCK, stride=PITCH), :] = self.row_recv(step, 1)[
                        pl.ds(at, BLOCK), :
                    ]
                for dl in range(BLOCK):
                    level = first + dl
                    e = jnp.where(polar_mask, zero, horiz[step, 0, level])
                    w = jnp.where(polar_mask, zero, horiz[step, 1, level])
                    n = jnp.where(global_row == n_lat * lats - 1, zero, horiz[step, 2, level])
                    s = jnp.where(global_row == 0, zero, horiz[step, 3, level])
                    keep = 1.0 - e - w - n - s
                    edge = jnp.where(lane == lons - 1, e, jnp.where(lane == 0, w, zero))
                    e = jnp.where(lane == lons - 1, zero, e)
                    w = jnp.where(lane == 0, zero, w)
                    for t in range(count):
                        start = pl.multiple_of(self.base(t, level), 8)
                        here = padded[pl.ds(start, lats), :]
                        k = dl * count + t
                        field[self.tile(t, level), :] = (
                            keep * here
                            + e * pltpu.roll(here, lons - 1, 1)
                            + w * pltpu.roll(here, 1, 1)
                            + edge * pltpu.roll(halo, lons - 1 - 2 * k, 1)
                            + n * padded[pl.ds(start + 1, lats), :]
                            + s * padded[pl.ds(start - 1, lats), :]
                        )
                return carry

            lax.fori_loop(0, blocks, block, 0)

        def begin(self, step):
            self.vertical(step)
            self.release(step)
            self.pole_local(step)

        def end(self, step):
            self.receive(step)
            self.pole_finish(step)
            self.horizontal(step)

        def drain(self):
            for step in range(STEPS):
                for side in range(2):
                    self.row_copy(step, side).wait_send()
                    self.col_copy(step, side).wait_send()

                @pl.when(is_polar)
                def _():
                    for d in range(1, n_lon):
                        self.pole_copy(step, d).wait_send()

    def main(g):
        return Part(
            g * GROUP,
            GROUP,
            g,
            (
                lambda step, side: row_send.at[step, side, g],
                lambda step, side: row_recv.at[step, side, g],
                lambda step: col_send.at[step, g],
                lambda step, side: col_recv.at[step, side, g],
                lambda step: pole_send.at[step, g],
                lambda step: pole_recv.at[step, g],
                lambda step: pole_part.at[g],
            ),
        )

    extra = Part(
        tracers,
        1,
        groups,
        (
            lambda step, side: extra_row_send.at[step, side],
            lambda step, side: extra_row_recv.at[step, side],
            lambda step: extra_col_send.at[step],
            lambda step, side: extra_col_recv.at[step, side],
            lambda step: extra_pole_send.at[step],
            lambda step: extra_pole_recv.at[step],
            lambda step: extra_pole_part,
        ),
    )

    def over(lo, hi, body):
        def turn(g, carry):
            body(g)
            return carry

        lax.fori_loop(lo, hi, turn, 0)

    slab = GROUP * levels * lats

    def out_copy(g):
        rows = pl.ds(pl.multiple_of(g * slab, slab), slab)
        return pltpu.make_async_copy(field.at[rows], out_hbm.at[rows], out_sem.at[g])

    def middle(g):
        part = main(g)
        part.end(1)
        part.begin(0)

    def last(g):
        main(g).end(0)
        out_copy(g).start()

    load_vert.wait()
    load_field.wait()
    over(0, groups, lambda g: main(g).begin(1))
    forward()
    load_horiz.wait()
    over(0, groups, middle)
    collect()
    extra.begin(1)
    over(0, 1, last)
    extra.end(1)
    extra.begin(0)
    over(1, groups, last)
    extra.end(0)
    extra_copy = pltpu.make_async_copy(
        field.at[pl.ds(extra_base, levels * lats)], extra_hbm, out_sem.at[groups]
    )
    extra_copy.start()

    for d in range(1, n_lat):
        first_copy(d).wait_send()
    for d in range(1, n_lon):
        second_copy(d).wait_send()
    over(0, groups, lambda g: main(g).drain())
    extra.drain()
    over(0, groups, lambda g: out_copy(g).wait())
    extra_copy.wait()


def transport(mesh_shape, adjoint_in, horiz_frac, vert_frac, shift, frac, sound, cols, counts):
    tracers, levels, lats, lons = adjoint_in.shape
    n_lat, n_lon = mesh_shape
    senders, slots = cols.shape
    groups = tracers // GROUP
    blocks = levels // BLOCK
    per_group = GROUP * levels
    features = sound.shape[1]
    f32 = jnp.float32
    any_spec = pl.BlockSpec(memory_space=pl.ANY)
    vmem = pl.BlockSpec(memory_space=pltpu.VMEM)
    smem = pl.BlockSpec(memory_space=pltpu.SMEM)
    dma = pltpu.SemaphoreType.DMA
    rows = tracers * levels * lats
    out, extra = pl.pallas_call(
        functools.partial(kernel, (tracers, levels, lats, lons, n_lat, n_lon, slots)),
        out_shape=(
            jax.ShapeDtypeStruct((rows, lons), f32),
            jax.ShapeDtypeStruct((levels * lats, lons), f32),
        ),
        in_specs=[smem, smem, any_spec, any_spec, any_spec, any_spec, vmem, vmem],
        out_specs=(any_spec, any_spec),
        scratch_shapes=[
            pltpu.VMEM((rows + levels * lats, lons), f32),
            pltpu.VMEM(horiz_frac.shape, f32),
            pltpu.VMEM(vert_frac.shape, f32),
            pltpu.VMEM(((tracers + 1) * levels * PITCH + 32, lons), f32),
            pltpu.VMEM((slots * senders, lons), jnp.int32),
            pltpu.VMEM((3 * (levels + 8), slots * senders), jnp.bfloat16),
            pltpu.VMEM((features, senders), f32),
            pltpu.VMEM((n_lat, n_lon, features), f32),
            pltpu.VMEM((senders * features // lons, lons), f32),
            pltpu.VMEM((senders * features // lons, lons), f32),
            pltpu.VMEM((STEPS, 2, groups, per_group, lons), f32),
            pltpu.VMEM((STEPS, 2, groups, per_group, lons), f32),
            pltpu.VMEM((STEPS, groups, blocks, lats, lons), f32),
            pltpu.VMEM((STEPS, 2, groups, blocks, lats, lons), f32),
            pltpu.VMEM((STEPS, groups, lats, lons), f32),
            pltpu.VMEM((STEPS, groups, n_lon, lats, lons), f32),
            pltpu.VMEM((groups, NPOLE, per_group, lons), f32),
            pltpu.VMEM((STEPS, 2, levels, lons), f32),
            pltpu.VMEM((STEPS, 2, levels, lons), f32),
            pltpu.VMEM((STEPS, blocks, lats, lons), f32),
            pltpu.VMEM((STEPS, 2, blocks, lats, lons), f32),
            pltpu.VMEM((STEPS, lats, lons), f32),
            pltpu.VMEM((STEPS, n_lon, lats, lons), f32),
            pltpu.VMEM((NPOLE, levels, lons), f32),
            pltpu.VMEM((STEPS, NPOLE, 3 * lons, lons), jnp.bfloat16),
            dma((4,)),
            dma((groups + 1,)),
            dma((n_lat,)),
            dma((n_lat,)),
            dma((n_lon,)),
            dma((n_lon,)),
            dma((STEPS, 2, groups + 1)),
            dma((STEPS, 2, groups + 1)),
            dma((STEPS, 2, groups + 1)),
            dma((STEPS, 2, groups + 1)),
            dma((STEPS, groups + 1, n_lon)),
            dma((STEPS, groups + 1, n_lon)),
        ],
        compiler_params=pltpu.CompilerParams(
            collective_id=0, has_side_effects=True, vmem_limit_bytes=60 * 1024 * 1024
        ),
    )(shift, frac, adjoint_in.reshape(rows, lons), horiz_frac, vert_frac, sound, cols, counts)
    return out.reshape(adjoint_in.shape) + extra.reshape(levels, lats, lons)[None]


def solution(mesh):
    mesh_shape = (mesh.shape["lat"], mesh.shape["lon"])

    def on_device(
        adjoint_in,
        horiz_frac,
        vert_frac,
        polar_shift,
        polar_frac,
        sound_forcing,
        sound_col,
        sound_count,
    ):
        return transport(
            mesh_shape,
            adjoint_in,
            horiz_frac,
            vert_frac,
            polar_shift,
            polar_frac,
            sound_forcing[0],
            sound_col[0],
            sound_count,
        )

    return jax.shard_map(
        on_device,
        mesh=mesh,
        in_specs=(
            P(None, None, "lat", "lon"),
            P(None, None, None, "lat", "lon"),
            P(None, None, None, "lat", "lon"),
            P(),
            P(),
            P(("lat", "lon"), None, None),
            P(("lat", "lon"), None, None),
            P(("lat", "lon"), None),
        ),
        out_specs=P(None, None, "lat", "lon"),
        check_vma=False,
    )
```

```python
import functools

import jax
import jax.numpy as jnp
from jax import lax
from jax.experimental import pallas as pl
from jax.experimental.pallas import tpu as pltpu
from jax.sharding import PartitionSpec as P

MESH = pl.DeviceIdType.MESH
NPOLE = 2
STEPS = 2
GROUP = 4
PITCH = 16
BLOCK = 8
VMEM_LIMIT = 33 * 1024 * 1024


def log_of(value):
    shifted = value - 1.0
    z = shifted / (2.0 + shifted)
    square = z * z
    total = jnp.full_like(z, 1.0 / 17.0)
    for odd in (15, 13, 11, 9, 7, 5, 3, 1):
        total = total * square + 1.0 / odd
    return 2.0 * z * total


def halves(value):
    high = value.astype(jnp.bfloat16)
    return high, (value - high.astype(jnp.float32)).astype(jnp.bfloat16)


def kernel(
    sizes,
    shift_ref,
    frac_ref,
    adjoint_hbm,
    horiz_hbm,
    vert_hbm,
    sound_hbm,
    col_ref,
    count_ref,
    out_hbm,
    extra_hbm,
    field,
    horiz,
    vert,
    padded,
    owned,
    parts,
    turned,
    first_recv,
    second_send,
    second_recv,
    row_send,
    row_recv,
    col_send,
    col_recv,
    pole_send,
    pole_recv,
    pole_part,
    extra_row_send,
    extra_row_recv,
    extra_col_send,
    extra_col_recv,
    extra_pole_send,
    extra_pole_recv,
    extra_pole_part,
    pole_matrix,
    load_sem,
    out_sem,
    first_send_sem,
    first_recv_sem,
    second_send_sem,
    second_recv_sem,
    row_send_sem,
    row_recv_sem,
    col_send_sem,
    col_recv_sem,
    pole_send_sem,
    pole_recv_sem,
):
    tracers, levels, lats, lons, n_lat, n_lon, slots = sizes
    groups = tracers // GROUP
    blocks = levels // BLOCK
    senders = n_lat * n_lon
    chunks = slots * levels // lons
    lat = lax.axis_index("lat")
    lon = lax.axis_index("lon")
    north = lax.rem(lat + 1, n_lat)
    south = lax.rem(lat + n_lat - 1, n_lat)
    east = lax.rem(lon + 1, n_lon)
    west = lax.rem(lon + n_lon - 1, n_lon)
    at_top = lat == 0
    is_polar = at_top | (lat == n_lat - 1)
    pole_row = jnp.where(at_top, 0, lats - NPOLE)
    first_pole = jnp.where(at_top, 0, NPOLE)

    lane = lax.broadcasted_iota(jnp.int32, (lats, lons), 1)
    sub = lax.broadcasted_iota(jnp.int32, (lats, lons), 0)

    volume = tracers * levels * lats
    load_vert = pltpu.make_async_copy(vert_hbm, vert, load_sem.at[0])
    load_field = pltpu.make_async_copy(adjoint_hbm, field.at[pl.ds(0, volume)], load_sem.at[1])
    load_horiz = pltpu.make_async_copy(horiz_hbm, horiz, load_sem.at[2])
    load_own = pltpu.make_async_copy(
        sound_hbm.at[pl.ds(lat * n_lon, n_lon)], first_recv.at[lat], load_sem.at[3]
    )
    load_vert.start()
    load_field.start()
    load_horiz.start()
    load_own.start()

    barrier = pltpu.get_barrier_semaphore()
    for d in range(1, n_lat):
        pl.semaphore_signal(
            barrier, inc=1, device_id=(lax.rem(lat + d, n_lat), lon), device_id_type=MESH
        )
    for d in range(1, n_lon):
        pl.semaphore_signal(
            barrier, inc=1, device_id=(lat, lax.rem(lon + d, n_lon)), device_id_type=MESH
        )

    def courant(step, p):
        return shift_ref[step, first_pole + p].astype(jnp.float32) + frac_ref[step, first_pole + p]

    def log_retain(step, p, shape):
        c = jnp.full(shape, courant(step, p), jnp.float32)
        return log_of(c / (1.0 + c))

    @pl.when(is_polar)
    def _():
        j = lax.broadcasted_iota(jnp.int32, (lons, lons), 0)
        i = lax.broadcasted_iota(jnp.int32, (lons, lons), 1)
        distance = (j - i).astype(jnp.float32)
        for step in range(STEPS):
            for p in range(NPOLE):
                power = jnp.exp(jnp.maximum(distance, 0.0) * log_retain(step, p, (lons, lons)))
                weight = 1.0 / (1.0 + jnp.full((lons, lons), courant(step, p), jnp.float32))
                matrix = jnp.where(distance >= 0.0, power, 0.0) * weight
                high, low = halves(matrix)
                pole_matrix[step, p, 0:lons, :] = high
                pole_matrix[step, p, lons : 2 * lons, :] = high
                pole_matrix[step, p, 2 * lons : 3 * lons, :] = low

    slot = lax.broadcasted_iota(jnp.int32, (slots, senders), 0)
    filled = jnp.where(slot < count_ref[...], col_ref[...], -1)
    columns = jnp.concatenate([filled] * (senders // slots), axis=0).T
    for j in range(slots):
        spread = jnp.broadcast_to(columns[:, j : j + 1], (senders, lons))
        for a in range(n_lat):
            owned[pl.ds(j * senders + a, n_lon, stride=n_lat), :] = spread[
                a * n_lon : (a + 1) * n_lon
            ]

    pl.semaphore_wait(barrier, n_lat + n_lon - 2)

    def first_copy(d):
        target = lax.rem(lat + d, n_lat)
        return pltpu.make_async_remote_copy(
            src_ref=sound_hbm.at[pl.ds(target * n_lon, n_lon)],
            dst_ref=first_recv.at[lat],
            send_sem=first_send_sem.at[d],
            recv_sem=first_recv_sem.at[lat],
            device_id=(target, lon),
            device_id_type=MESH,
        )

    def first_arrival(d):
        source = lax.rem(lat + d, n_lat)
        return pltpu.make_async_remote_copy(
            src_ref=first_recv.at[source],
            dst_ref=first_recv.at[source],
            send_sem=first_send_sem.at[d],
            recv_sem=first_recv_sem.at[source],
            device_id=(source, lon),
            device_id_type=MESH,
        )

    share = chunks * n_lat

    def second_copy(d):
        target = lax.rem(lon + d, n_lon)
        return pltpu.make_async_remote_copy(
            src_ref=second_send.at[pl.ds(target * share, share)],
            dst_ref=second_recv.at[pl.ds(lon * share, share)],
            send_sem=second_send_sem.at[d],
            recv_sem=second_recv_sem.at[lon],
            device_id=(lat, target),
            device_id_type=MESH,
        )

    def second_arrival(d):
        source = lax.rem(lon + d, n_lon)
        here = second_recv.at[pl.ds(source * share, share)]
        return pltpu.make_async_remote_copy(
            src_ref=here,
            dst_ref=here,
            send_sem=second_send_sem.at[d],
            recv_sem=second_recv_sem.at[source],
            device_id=(lat, source),
            device_id_type=MESH,
        )

    second_own = pltpu.make_async_copy(
        second_send.at[pl.ds(lon * share, share)],
        second_recv.at[pl.ds(lon * share, share)],
        second_recv_sem.at[lon],
    )

    for d in range(1, n_lat):
        first_copy(d).start()

    def forward():
        load_own.wait()
        for d in range(1, n_lat):
            first_arrival(d).wait_recv()
        for a in range(n_lat):
            for half in range(n_lon // 8):
                for i in range(chunks):
                    second_send[pl.ds((half * 8 * chunks + i) * n_lat + a, 8, stride=share), :] = (
                        first_recv[a, half * 8 : half * 8 + 8, i * lons : (i + 1) * lons]
                    )
        for d in range(1, n_lon):
            second_copy(d).start()
        second_own.start()

    extra_base = tracers * levels * lats

    def collect():
        second_own.wait()
        for d in range(1, n_lon):
            second_arrival(d).wait_recv()
        for i in range(chunks):
            rows = [
                second_recv[(b * chunks + i) * n_lat : (b * chunks + i + 1) * n_lat, :]
                for b in range(n_lon)
            ]
            turned[i * lons : (i + 1) * lons, :] = jnp.concatenate(rows, axis=0).T
        gap = jnp.zeros((8, senders), jnp.float32)
        for j in range(slots):
            piece = turned[j * levels : (j + 1) * levels, :]
            high = piece.astype(jnp.bfloat16).astype(jnp.float32)
            rest = piece - high
            middle = rest.astype(jnp.bfloat16).astype(jnp.float32)
            low = rest - middle
            stacked = jnp.concatenate([high, gap, middle, gap, low, gap], axis=0)
            parts[:, j * senders : (j + 1) * senders] = stacked.astype(jnp.bfloat16)
        span = levels + 8

        def place(pair, carry):
            here = lax.broadcasted_iota(jnp.int32, (slots * senders, lons), 1) + pair * (2 * lons)
            cols = owned[...]
            hot = jnp.concatenate(
                [
                    jnp.where(cols == here, 1.0, 0.0).astype(jnp.bfloat16),
                    jnp.where(cols == here + lons, 1.0, 0.0).astype(jnp.bfloat16),
                ],
                axis=1,
            )
            got = jnp.dot(parts[...], hot, preferred_element_type=jnp.float32)
            total = got[:levels] + got[span : span + levels] + got[2 * span : 2 * span + levels]
            field[pl.ds(extra_base + 2 * pair, levels, stride=lats), :] = total[:, :lons]
            field[pl.ds(extra_base + 2 * pair + 1, levels, stride=lats), :] = total[:, lons:]
            return carry

        lax.fori_loop(0, lats // 2, place, 0)

    pair_index = ((lane + 1) >> 1) & (lons // 2 - 1)
    global_row = lat * lats + sub
    polar_mask = (global_row < NPOLE) | (global_row >= n_lat * lats - NPOLE)
    zero = jnp.zeros((lats, lons), jnp.float32)

    class Part:
        def __init__(self, first, count, index, buffers):
            self.first, self.count, self.index = first, count, index
            self.extra = index == groups if isinstance(index, int) else False
            (
                self.row_send,
                self.row_recv,
                self.col_send,
                self.col_recv,
                self.pole_send,
                self.pole_recv,
                self.pole_part,
            ) = buffers

        def base(self, t, level):
            return ((self.first + t) * levels + level) * PITCH + 8

        def tile(self, t, level):
            return pl.ds(pl.multiple_of(((self.first + t) * levels + level) * lats, lats), lats)

        def vertical(self, step):
            count = self.count

            def block(lb, carry):
                first = lb * BLOCK
                before = jnp.maximum(first - 1, 0)
                down_tiles = [field[self.tile(t, before), :] for t in range(count)]
                here_tiles = [field[self.tile(t, first), :] for t in range(count)]
                packed = zero
                for dl in range(BLOCK):
                    level = first + dl
                    after = jnp.minimum(level + 1, levels - 1)
                    up = vert[step, 0, level]
                    down = vert[step, 1, level]
                    keep = 1.0 - up - down
                    for t in range(count):
                        up_tile = field[self.tile(t, after), :]
                        mixed = keep * here_tiles[t] + up * up_tile + down * down_tiles[t]
                        start = pl.multiple_of(self.base(t, level), 8)
                        padded[pl.ds(start, lats), :] = mixed
                        k = dl * count + t
                        turn = mixed if k == 0 else pltpu.roll(mixed, 2 * k, 1)
                        packed = jnp.where(pair_index == k, turn, packed)
                        down_tiles[t] = here_tiles[t]
                        here_tiles[t] = up_tile
                self.col_send(step)[lb] = packed
                for t in range(count):
                    start = self.base(t, first)
                    to = pl.multiple_of(t * levels + first, 8)
                    self.row_send(step, 0)[pl.ds(to, BLOCK), :] = padded[
                        pl.ds(start, BLOCK, stride=PITCH), :
                    ]
                    self.row_send(step, 1)[pl.ds(to, BLOCK), :] = padded[
                        pl.ds(start + lats - 1, BLOCK, stride=PITCH), :
                    ]
                return carry

            lax.fori_loop(0, blocks, block, 0)

        def row_copy(self, step, side):
            return pltpu.make_async_remote_copy(
                src_ref=self.row_send(step, side),
                dst_ref=self.row_recv(step, side),
                send_sem=row_send_sem.at[step, side, self.index],
                recv_sem=row_recv_sem.at[step, side, self.index],
                device_id=(south, lon) if side == 0 else (north, lon),
                device_id_type=MESH,
            )

        def col_copy(self, step, side):
            return pltpu.make_async_remote_copy(
                src_ref=self.col_send(step),
                dst_ref=self.col_recv(step, side),
                send_sem=col_send_sem.at[step, side, self.index],
                recv_sem=col_recv_sem.at[step, side, self.index],
                device_id=(lat, west) if side == 0 else (lat, east),
                device_id_type=MESH,
            )

        def pole_copy(self, step, d):
            return pltpu.make_async_remote_copy(
                src_ref=self.pole_send(step),
                dst_ref=self.pole_recv(step).at[n_lon - d],
                send_sem=pole_send_sem.at[step, self.index, d],
                recv_sem=pole_recv_sem.at[step, self.index, n_lon - d],
                device_id=(lat, lax.rem(lon + d, n_lon)),
                device_id_type=MESH,
            )

        def release(self, step):
            for side in range(2):
                self.row_copy(step, side).start()
                self.col_copy(step, side).start()

        def receive(self, step):
            for side in range(2):
                self.row_copy(step, side).wait_recv()
                self.col_copy(step, side).wait_recv()

        def pole_local(self, step):
            count = self.count

            @pl.when(is_polar)
            def _():
                packed = zero
                for p in range(NPOLE):
                    start = self.base(0, 0) + pole_row + p
                    rows = padded[pl.ds(start, count * levels, stride=PITCH), :]
                    high, low = halves(rows)
                    solved = jnp.dot(
                        jnp.concatenate([high, low, high], axis=1),
                        pole_matrix[step, p],
                        preferred_element_type=jnp.float32,
                    )
                    self.pole_part(step)[p] = solved
                    for q in range(count * blocks):
                        tile = solved[q * 8 : q * 8 + 8]
                        at = p * count * blocks + q
                        turn = tile if at == 0 else pltpu.roll(tile, at, 1)
                        packed = jnp.where(lane == at, turn, packed)
                self.pole_send(step)[...] = packed
                for d in range(1, n_lon):
                    self.pole_copy(step, d).start()

        def pole_finish(self, step):
            count = self.count

            @pl.when(is_polar)
            def _():
                for d in range(1, n_lon):
                    self.pole_copy(step, d).wait_recv()
                logs = [log_retain(step, p, (lats, lons)) for p in range(NPOLE)]
                log = jnp.where(lane < count * blocks, logs[0], logs[1])
                inflow = self.pole_send(step)[...] * jnp.exp((float(lons) * (n_lon - 1)) * log)
                for d in range(1, n_lon):
                    inflow = inflow + self.pole_recv(step)[d] * jnp.exp(
                        (float(lons) * (d - 1)) * log
                    )
                inflow = inflow / (1.0 - jnp.exp(float(lons * n_lon) * log))
                for p in range(NPOLE):
                    carried = jnp.exp((lons - lane).astype(jnp.float32) * logs[p])
                    for q in range(count * blocks):
                        at = p * count * blocks + q
                        start = self.base(0, q * BLOCK) + pole_row + p
                        spread = jnp.broadcast_to(inflow[:, at : at + 1], (lats, lons))
                        padded[pl.ds(start, BLOCK, stride=PITCH), :] = (
                            self.pole_part(step)[p, q * 8 : q * 8 + 8, :] + carried * spread
                        )

        def horizontal(self, step):
            count = self.count

            def block(lb, carry):
                first = lb * BLOCK
                halo = jnp.where(
                    (lane & 1) == 0,
                    self.col_recv(step, 0)[lb],
                    pltpu.roll(self.col_recv(step, 1)[lb], 2, 1),
                )
                for t in range(count):
                    start = self.base(t, first)
                    at = pl.multiple_of(t * levels + first, 8)
                    padded[pl.ds(start + lats, BLOCK, stride=PITCH), :] = self.row_recv(step, 0)[
                        pl.ds(at, BLOCK), :
                    ]
                    padded[pl.ds(start - 1, BLOCK, stride=PITCH), :] = self.row_recv(step, 1)[
                        pl.ds(at, BLOCK), :
                    ]
                for dl in range(BLOCK):
                    level = first + dl
                    e = jnp.where(polar_mask, zero, horiz[step, 0, level])
                    w = jnp.where(polar_mask, zero, horiz[step, 1, level])
                    n = jnp.where(global_row == n_lat * lats - 1, zero, horiz[step, 2, level])
                    s = jnp.where(global_row == 0, zero, horiz[step, 3, level])
                    keep = 1.0 - e - w - n - s
                    edge = jnp.where(lane == lons - 1, e, jnp.where(lane == 0, w, zero))
                    e = jnp.where(lane == lons - 1, zero, e)
                    w = jnp.where(lane == 0, zero, w)
                    for t in range(count):
                        start = pl.multiple_of(self.base(t, level), 8)
                        here = padded[pl.ds(start, lats), :]
                        k = dl * count + t
                        field[self.tile(t, level), :] = (
                            keep * here
                            + e * pltpu.roll(here, lons - 1, 1)
                            + w * pltpu.roll(here, 1, 1)
                            + edge * pltpu.roll(halo, lons - 1 - 2 * k, 1)
                            + n * padded[pl.ds(start + 1, lats), :]
                            + s * padded[pl.ds(start - 1, lats), :]
                        )
                return carry

            lax.fori_loop(0, blocks, block, 0)

        def begin(self, step):
            self.vertical(step)
            self.release(step)
            self.pole_local(step)

        def end(self, step):
            self.receive(step)
            self.pole_finish(step)
            self.horizontal(step)

        def drain(self):
            for step in range(STEPS):
                for side in range(2):
                    self.row_copy(step, side).wait_send()
                    self.col_copy(step, side).wait_send()

                @pl.when(is_polar)
                def _():
                    for d in range(1, n_lon):
                        self.pole_copy(step, d).wait_send()

    def main(g):
        return Part(
            g * GROUP,
            GROUP,
            g,
            (
                lambda step, side: row_send.at[step, side, g],
                lambda step, side: row_recv.at[step, side, g],
                lambda step: col_send.at[step, g],
                lambda step, side: col_recv.at[step, side, g],
                lambda step: pole_send.at[step, g],
                lambda step: pole_recv.at[step, g],
                lambda step: pole_part.at[g],
            ),
        )

    extra = Part(
        tracers,
        1,
        groups,
        (
            lambda step, side: extra_row_send.at[step, side],
            lambda step, side: extra_row_recv.at[step, side],
            lambda step: extra_col_send.at[step],
            lambda step, side: extra_col_recv.at[step, side],
            lambda step: extra_pole_send.at[step],
            lambda step: extra_pole_recv.at[step],
            lambda step: extra_pole_part,
        ),
    )

    def over(lo, hi, body):
        def turn(g, carry):
            body(g)
            return carry

        lax.fori_loop(lo, hi, turn, 0)

    slab = GROUP * levels * lats

    def out_copy(g):
        rows = pl.ds(pl.multiple_of(g * slab, slab), slab)
        return pltpu.make_async_copy(field.at[rows], out_hbm.at[rows], out_sem.at[g])

    def middle(g):
        part = main(g)
        part.end(1)
        part.begin(0)

    def last(g):
        main(g).end(0)
        out_copy(g).start()

    load_vert.wait()
    load_field.wait()
    over(0, groups, lambda g: main(g).begin(1))
    forward()
    load_horiz.wait()
    over(0, groups, middle)
    collect()
    extra.begin(1)
    over(0, 1, last)
    extra.end(1)
    extra.begin(0)
    over(1, groups, last)
    extra.end(0)
    extra_copy = pltpu.make_async_copy(
        field.at[pl.ds(extra_base, levels * lats)], extra_hbm, out_sem.at[groups]
    )
    extra_copy.start()

    for d in range(1, n_lat):
        first_copy(d).wait_send()
    for d in range(1, n_lon):
        second_copy(d).wait_send()
    over(0, groups, lambda g: main(g).drain())
    extra.drain()
    over(0, groups, lambda g: out_copy(g).wait())
    extra_copy.wait()


def stay(array):
    return pltpu.with_memory_space_constraint(array, pltpu.HBM)


def transport(mesh_shape, adjoint_in, horiz_frac, vert_frac, shift, frac, sound, cols, counts):
    tracers, levels, lats, lons = adjoint_in.shape
    n_lat, n_lon = mesh_shape
    slots, senders = cols.shape
    groups = tracers // GROUP
    blocks = levels // BLOCK
    per_group = GROUP * levels
    features = sound.shape[1]
    f32 = jnp.float32
    any_spec = pl.BlockSpec(memory_space=pl.ANY)
    hbm = pl.BlockSpec(memory_space=pltpu.HBM)
    vmem = pl.BlockSpec(memory_space=pltpu.VMEM)
    smem = pl.BlockSpec(memory_space=pltpu.SMEM)
    dma = pltpu.SemaphoreType.DMA
    rows = tracers * levels * lats
    out, extra = pl.pallas_call(
        functools.partial(kernel, (tracers, levels, lats, lons, n_lat, n_lon, slots)),
        out_shape=(
            jax.ShapeDtypeStruct((rows, lons), f32),
            jax.ShapeDtypeStruct((levels * lats, lons), f32),
        ),
        in_specs=[smem, smem, hbm, hbm, hbm, hbm, vmem, vmem],
        out_specs=(any_spec, any_spec),
        scratch_shapes=[
            pltpu.VMEM((rows + levels * lats, lons), f32),
            pltpu.VMEM(horiz_frac.shape, f32),
            pltpu.VMEM(vert_frac.shape, f32),
            pltpu.VMEM(((tracers + 1) * levels * PITCH + 32, lons), f32),
            pltpu.VMEM((slots * senders, lons), jnp.int32),
            pltpu.VMEM((3 * (levels + 8), slots * senders), jnp.bfloat16),
            pltpu.VMEM((features, senders), f32),
            pltpu.VMEM((n_lat, n_lon, features), f32),
            pltpu.VMEM((senders * features // lons, lons), f32),
            pltpu.VMEM((senders * features // lons, lons), f32),
            pltpu.VMEM((STEPS, 2, groups, per_group, lons), f32),
            pltpu.VMEM((STEPS, 2, groups, per_group, lons), f32),
            pltpu.VMEM((STEPS, groups, blocks, lats, lons), f32),
            pltpu.VMEM((STEPS, 2, groups, blocks, lats, lons), f32),
            pltpu.VMEM((STEPS, groups, lats, lons), f32),
            pltpu.VMEM((STEPS, groups, n_lon, lats, lons), f32),
            pltpu.VMEM((groups, NPOLE, per_group, lons), f32),
            pltpu.VMEM((STEPS, 2, levels, lons), f32),
            pltpu.VMEM((STEPS, 2, levels, lons), f32),
            pltpu.VMEM((STEPS, blocks, lats, lons), f32),
            pltpu.VMEM((STEPS, 2, blocks, lats, lons), f32),
            pltpu.VMEM((STEPS, lats, lons), f32),
            pltpu.VMEM((STEPS, n_lon, lats, lons), f32),
            pltpu.VMEM((NPOLE, levels, lons), f32),
            pltpu.VMEM((STEPS, NPOLE, 3 * lons, lons), jnp.bfloat16),
            dma((4,)),
            dma((groups + 1,)),
            dma((n_lat,)),
            dma((n_lat,)),
            dma((n_lon,)),
            dma((n_lon,)),
            dma((STEPS, 2, groups + 1)),
            dma((STEPS, 2, groups + 1)),
            dma((STEPS, 2, groups + 1)),
            dma((STEPS, 2, groups + 1)),
            dma((STEPS, groups + 1, n_lon)),
            dma((STEPS, groups + 1, n_lon)),
        ],
        compiler_params=pltpu.CompilerParams(
            collective_id=0, has_side_effects=True, vmem_limit_bytes=VMEM_LIMIT
        ),
    )(
        stay(shift),
        stay(frac),
        stay(adjoint_in.reshape(rows, lons)),
        stay(horiz_frac),
        stay(vert_frac),
        stay(sound),
        stay(cols),
        stay(counts),
    )
    return out.reshape(adjoint_in.shape) + extra.reshape(levels, lats, lons)[None]


def solution(mesh):
    mesh_shape = (mesh.shape["lat"], mesh.shape["lon"])

    def on_device(
        adjoint_in,
        horiz_frac,
        vert_frac,
        polar_shift,
        polar_frac,
        sound_forcing,
        sound_col,
        sound_count,
    ):
        return transport(
            mesh_shape,
            adjoint_in,
            horiz_frac,
            vert_frac,
            polar_shift,
            polar_frac,
            sound_forcing[0],
            sound_col[0].T,
            sound_count,
        )

    return jax.shard_map(
        on_device,
        mesh=mesh,
        in_specs=(
            P(None, None, "lat", "lon"),
            P(None, None, None, "lat", "lon"),
            P(None, None, None, "lat", "lon"),
            P(),
            P(),
            P(("lat", "lon"), None, None),
            P(("lat", "lon"), None, None),
            P(("lat", "lon"), None),
        ),
        out_specs=P(None, None, "lat", "lon"),
        check_vma=False,
    )
```

```python
import functools

import jax
import jax.numpy as jnp
from jax import lax
from jax.experimental import pallas as pl
from jax.experimental.pallas import tpu as pltpu
from jax.sharding import PartitionSpec as P

MESH = pl.DeviceIdType.MESH
NPOLE = 2
STEPS = 2
GROUP = 4
PITCH = 16
BLOCK = 8
VMEM_LIMIT = 33 * 1024 * 1024


def log_of(value):
    shifted = value - 1.0
    z = shifted / (2.0 + shifted)
    square = z * z
    total = jnp.full_like(z, 1.0 / 17.0)
    for odd in (15, 13, 11, 9, 7, 5, 3, 1):
        total = total * square + 1.0 / odd
    return 2.0 * z * total


def halves(value):
    high = value.astype(jnp.bfloat16)
    return high, (value - high.astype(jnp.float32)).astype(jnp.bfloat16)


def kernel(
    sizes,
    shift_ref,
    frac_ref,
    adjoint_hbm,
    horiz_hbm,
    vert_hbm,
    sound_hbm,
    col_ref,
    count_ref,
    out_hbm,
    extra_hbm,
    field,
    horiz,
    vert,
    padded,
    owned,
    parts,
    turned,
    first_recv,
    second_send,
    second_recv,
    row_send,
    row_recv,
    col_send,
    col_recv,
    pole_send,
    pole_recv,
    pole_part,
    extra_row_send,
    extra_row_recv,
    extra_col_send,
    extra_col_recv,
    extra_pole_send,
    extra_pole_recv,
    extra_pole_part,
    pole_matrix,
    load_sem,
    out_sem,
    first_send_sem,
    first_recv_sem,
    second_send_sem,
    second_recv_sem,
    row_send_sem,
    row_recv_sem,
    col_send_sem,
    col_recv_sem,
    pole_send_sem,
    pole_recv_sem,
):
    tracers, levels, lats, lons, n_lat, n_lon, slots = sizes
    groups = tracers // GROUP
    blocks = levels // BLOCK
    senders = n_lat * n_lon
    chunks = slots * levels // lons
    lat = lax.axis_index("lat")
    lon = lax.axis_index("lon")
    north = lax.rem(lat + 1, n_lat)
    south = lax.rem(lat + n_lat - 1, n_lat)
    east = lax.rem(lon + 1, n_lon)
    west = lax.rem(lon + n_lon - 1, n_lon)
    at_top = lat == 0
    is_polar = at_top | (lat == n_lat - 1)
    pole_row = jnp.where(at_top, 0, lats - NPOLE)
    first_pole = jnp.where(at_top, 0, NPOLE)

    lane = lax.broadcasted_iota(jnp.int32, (lats, lons), 1)
    sub = lax.broadcasted_iota(jnp.int32, (lats, lons), 0)

    slab = GROUP * levels * lats
    load_vert = pltpu.make_async_copy(vert_hbm, vert, load_sem.at[0])
    load_horiz = pltpu.make_async_copy(horiz_hbm, horiz, load_sem.at[1])
    load_own = pltpu.make_async_copy(
        sound_hbm.at[pl.ds(lat * n_lon, n_lon)], first_recv.at[lat], load_sem.at[2]
    )

    def load_slab(g):
        rows = pl.ds(pl.multiple_of(g * slab, slab), slab)
        return pltpu.make_async_copy(adjoint_hbm.at[rows], field.at[rows], load_sem.at[3 + g])

    load_vert.start()
    for g in range(groups):
        load_slab(g).start()
    load_own.start()

    barrier = pltpu.get_barrier_semaphore()
    for d in range(1, n_lat):
        pl.semaphore_signal(
            barrier, inc=1, device_id=(lax.rem(lat + d, n_lat), lon), device_id_type=MESH
        )
    for d in range(1, n_lon):
        pl.semaphore_signal(
            barrier, inc=1, device_id=(lat, lax.rem(lon + d, n_lon)), device_id_type=MESH
        )

    def courant(step, p):
        return shift_ref[step, first_pole + p].astype(jnp.float32) + frac_ref[step, first_pole + p]

    def log_retain(step, p, shape):
        c = jnp.full(shape, courant(step, p), jnp.float32)
        return log_of(c / (1.0 + c))

    @pl.when(is_polar)
    def _():
        j = lax.broadcasted_iota(jnp.int32, (lons, lons), 0)
        i = lax.broadcasted_iota(jnp.int32, (lons, lons), 1)
        distance = (j - i).astype(jnp.float32)
        for step in range(STEPS):
            for p in range(NPOLE):
                power = jnp.exp(jnp.maximum(distance, 0.0) * log_retain(step, p, (lons, lons)))
                weight = 1.0 / (1.0 + jnp.full((lons, lons), courant(step, p), jnp.float32))
                matrix = jnp.where(distance >= 0.0, power, 0.0) * weight
                high, low = halves(matrix)
                pole_matrix[step, p, 0:lons, :] = high
                pole_matrix[step, p, lons : 2 * lons, :] = high
                pole_matrix[step, p, 2 * lons : 3 * lons, :] = low

    slot = lax.broadcasted_iota(jnp.int32, (slots, senders), 0)
    filled = jnp.where(slot < count_ref[...], col_ref[...], -1)
    columns = jnp.concatenate([filled] * (senders // slots), axis=0).T
    for j in range(slots):
        spread = jnp.broadcast_to(columns[:, j : j + 1], (senders, lons))
        for a in range(n_lat):
            owned[pl.ds(j * senders + a, n_lon, stride=n_lat), :] = spread[
                a * n_lon : (a + 1) * n_lon
            ]

    pl.semaphore_wait(barrier, n_lat + n_lon - 2)

    def first_copy(d):
        target = lax.rem(lat + d, n_lat)
        return pltpu.make_async_remote_copy(
            src_ref=sound_hbm.at[pl.ds(target * n_lon, n_lon)],
            dst_ref=first_recv.at[lat],
            send_sem=first_send_sem.at[d],
            recv_sem=first_recv_sem.at[lat],
            device_id=(target, lon),
            device_id_type=MESH,
        )

    def first_arrival(d):
        source = lax.rem(lat + d, n_lat)
        return pltpu.make_async_remote_copy(
            src_ref=first_recv.at[source],
            dst_ref=first_recv.at[source],
            send_sem=first_send_sem.at[d],
            recv_sem=first_recv_sem.at[source],
            device_id=(source, lon),
            device_id_type=MESH,
        )

    share = chunks * n_lat

    def second_copy(d):
        target = lax.rem(lon + d, n_lon)
        return pltpu.make_async_remote_copy(
            src_ref=second_send.at[pl.ds(target * share, share)],
            dst_ref=second_recv.at[pl.ds(lon * share, share)],
            send_sem=second_send_sem.at[d],
            recv_sem=second_recv_sem.at[lon],
            device_id=(lat, target),
            device_id_type=MESH,
        )

    def second_arrival(d):
        source = lax.rem(lon + d, n_lon)
        here = second_recv.at[pl.ds(source * share, share)]
        return pltpu.make_async_remote_copy(
            src_ref=here,
            dst_ref=here,
            send_sem=second_send_sem.at[d],
            recv_sem=second_recv_sem.at[source],
            device_id=(lat, source),
            device_id_type=MESH,
        )

    second_own = pltpu.make_async_copy(
        second_send.at[pl.ds(lon * share, share)],
        second_recv.at[pl.ds(lon * share, share)],
        second_recv_sem.at[lon],
    )

    for d in range(1, n_lat):
        first_copy(d).start()

    def forward():
        load_own.wait()
        for d in range(1, n_lat):
            first_arrival(d).wait_recv()
        for a in range(n_lat):
            for half in range(n_lon // 8):
                for i in range(chunks):
                    second_send[pl.ds((half * 8 * chunks + i) * n_lat + a, 8, stride=share), :] = (
                        first_recv[a, half * 8 : half * 8 + 8, i * lons : (i + 1) * lons]
                    )
        for d in range(1, n_lon):
            second_copy(d).start()
        second_own.start()

    extra_base = tracers * levels * lats

    def collect():
        second_own.wait()
        for d in range(1, n_lon):
            second_arrival(d).wait_recv()
        for i in range(chunks):
            rows = [
                second_recv[(b * chunks + i) * n_lat : (b * chunks + i + 1) * n_lat, :]
                for b in range(n_lon)
            ]
            turned[i * lons : (i + 1) * lons, :] = jnp.concatenate(rows, axis=0).T
        gap = jnp.zeros((8, senders), jnp.float32)
        for j in range(slots):
            piece = turned[j * levels : (j + 1) * levels, :]
            high = piece.astype(jnp.bfloat16).astype(jnp.float32)
            rest = piece - high
            middle = rest.astype(jnp.bfloat16).astype(jnp.float32)
            low = rest - middle
            stacked = jnp.concatenate([high, gap, middle, gap, low, gap], axis=0)
            parts[:, j * senders : (j + 1) * senders] = stacked.astype(jnp.bfloat16)
        span = levels + 8

        def place(pair, carry):
            here = lax.broadcasted_iota(jnp.int32, (slots * senders, lons), 1) + pair * (2 * lons)
            cols = owned[...]
            hot = jnp.concatenate(
                [
                    jnp.where(cols == here, 1.0, 0.0).astype(jnp.bfloat16),
                    jnp.where(cols == here + lons, 1.0, 0.0).astype(jnp.bfloat16),
                ],
                axis=1,
            )
            got = jnp.dot(parts[...], hot, preferred_element_type=jnp.float32)
            total = got[:levels] + got[span : span + levels] + got[2 * span : 2 * span + levels]
            field[pl.ds(extra_base + 2 * pair, levels, stride=lats), :] = total[:, :lons]
            field[pl.ds(extra_base + 2 * pair + 1, levels, stride=lats), :] = total[:, lons:]
            return carry

        lax.fori_loop(0, lats // 2, place, 0)

    pair_index = ((lane + 1) >> 1) & (lons // 2 - 1)
    global_row = lat * lats + sub
    polar_mask = (global_row < NPOLE) | (global_row >= n_lat * lats - NPOLE)
    zero = jnp.zeros((lats, lons), jnp.float32)

    class Part:
        def __init__(self, first, count, index, buffers):
            self.first, self.count, self.index = first, count, index
            self.extra = index == groups if isinstance(index, int) else False
            (
                self.row_send,
                self.row_recv,
                self.col_send,
                self.col_recv,
                self.pole_send,
                self.pole_recv,
                self.pole_part,
            ) = buffers

        def base(self, t, level):
            return ((self.first + t) * levels + level) * PITCH + 8

        def tile(self, t, level):
            return pl.ds(pl.multiple_of(((self.first + t) * levels + level) * lats, lats), lats)

        def vertical(self, step):
            count = self.count

            def block(lb, carry):
                first = lb * BLOCK
                before = jnp.maximum(first - 1, 0)
                down_tiles = [field[self.tile(t, before), :] for t in range(count)]
                here_tiles = [field[self.tile(t, first), :] for t in range(count)]
                packed = zero
                for dl in range(BLOCK):
                    level = first + dl
                    after = jnp.minimum(level + 1, levels - 1)
                    up = vert[step, 0, level]
                    down = vert[step, 1, level]
                    keep = 1.0 - up - down
                    for t in range(count):
                        up_tile = field[self.tile(t, after), :]
                        mixed = keep * here_tiles[t] + up * up_tile + down * down_tiles[t]
                        start = pl.multiple_of(self.base(t, level), 8)
                        padded[pl.ds(start, lats), :] = mixed
                        k = dl * count + t
                        turn = mixed if k == 0 else pltpu.roll(mixed, 2 * k, 1)
                        packed = jnp.where(pair_index == k, turn, packed)
                        down_tiles[t] = here_tiles[t]
                        here_tiles[t] = up_tile
                self.col_send(step)[lb] = packed
                for t in range(count):
                    start = self.base(t, first)
                    to = pl.multiple_of(t * levels + first, 8)
                    self.row_send(step, 0)[pl.ds(to, BLOCK), :] = padded[
                        pl.ds(start, BLOCK, stride=PITCH), :
                    ]
                    self.row_send(step, 1)[pl.ds(to, BLOCK), :] = padded[
                        pl.ds(start + lats - 1, BLOCK, stride=PITCH), :
                    ]
                return carry

            lax.fori_loop(0, blocks, block, 0)

        def row_copy(self, step, side):
            return pltpu.make_async_remote_copy(
                src_ref=self.row_send(step, side),
                dst_ref=self.row_recv(step, side),
                send_sem=row_send_sem.at[step, side, self.index],
                recv_sem=row_recv_sem.at[step, side, self.index],
                device_id=(south, lon) if side == 0 else (north, lon),
                device_id_type=MESH,
            )

        def col_copy(self, step, side):
            return pltpu.make_async_remote_copy(
                src_ref=self.col_send(step),
                dst_ref=self.col_recv(step, side),
                send_sem=col_send_sem.at[step, side, self.index],
                recv_sem=col_recv_sem.at[step, side, self.index],
                device_id=(lat, west) if side == 0 else (lat, east),
                device_id_type=MESH,
            )

        def pole_copy(self, step, d):
            return pltpu.make_async_remote_copy(
                src_ref=self.pole_send(step),
                dst_ref=self.pole_recv(step).at[n_lon - d],
                send_sem=pole_send_sem.at[step, self.index, d],
                recv_sem=pole_recv_sem.at[step, self.index, n_lon - d],
                device_id=(lat, lax.rem(lon + d, n_lon)),
                device_id_type=MESH,
            )

        def release(self, step):
            for side in range(2):
                self.row_copy(step, side).start()
                self.col_copy(step, side).start()

        def receive(self, step):
            for side in range(2):
                self.row_copy(step, side).wait_recv()
                self.col_copy(step, side).wait_recv()

        def pole_local(self, step):
            count = self.count

            @pl.when(is_polar)
            def _():
                packed = zero
                for p in range(NPOLE):
                    start = self.base(0, 0) + pole_row + p
                    rows = padded[pl.ds(start, count * levels, stride=PITCH), :]
                    high, low = halves(rows)
                    solved = jnp.dot(
                        jnp.concatenate([high, low, high], axis=1),
                        pole_matrix[step, p],
                        preferred_element_type=jnp.float32,
                    )
                    self.pole_part(step)[p] = solved
                    for q in range(count * blocks):
                        tile = solved[q * 8 : q * 8 + 8]
                        at = p * count * blocks + q
                        turn = tile if at == 0 else pltpu.roll(tile, at, 1)
                        packed = jnp.where(lane == at, turn, packed)
                self.pole_send(step)[...] = packed
                for d in range(1, n_lon):
                    self.pole_copy(step, d).start()

        def pole_finish(self, step):
            count = self.count

            @pl.when(is_polar)
            def _():
                for d in range(1, n_lon):
                    self.pole_copy(step, d).wait_recv()
                logs = [log_retain(step, p, (lats, lons)) for p in range(NPOLE)]
                log = jnp.where(lane < count * blocks, logs[0], logs[1])
                inflow = self.pole_send(step)[...] * jnp.exp((float(lons) * (n_lon - 1)) * log)
                for d in range(1, n_lon):
                    inflow = inflow + self.pole_recv(step)[d] * jnp.exp(
                        (float(lons) * (d - 1)) * log
                    )
                inflow = inflow / (1.0 - jnp.exp(float(lons * n_lon) * log))
                for p in range(NPOLE):
                    carried = jnp.exp((lons - lane).astype(jnp.float32) * logs[p])
                    for q in range(count * blocks):
                        at = p * count * blocks + q
                        start = self.base(0, q * BLOCK) + pole_row + p
                        spread = jnp.broadcast_to(inflow[:, at : at + 1], (lats, lons))
                        padded[pl.ds(start, BLOCK, stride=PITCH), :] = (
                            self.pole_part(step)[p, q * 8 : q * 8 + 8, :] + carried * spread
                        )

        def horizontal(self, step):
            count = self.count

            def block(lb, carry):
                first = lb * BLOCK
                halo = jnp.where(
                    (lane & 1) == 0,
                    self.col_recv(step, 0)[lb],
                    pltpu.roll(self.col_recv(step, 1)[lb], 2, 1),
                )
                for t in range(count):
                    start = self.base(t, first)
                    at = pl.multiple_of(t * levels + first, 8)
                    padded[pl.ds(start + lats, BLOCK, stride=PITCH), :] = self.row_recv(step, 0)[
                        pl.ds(at, BLOCK), :
                    ]
                    padded[pl.ds(start - 1, BLOCK, stride=PITCH), :] = self.row_recv(step, 1)[
                        pl.ds(at, BLOCK), :
                    ]
                for dl in range(BLOCK):
                    level = first + dl
                    e = jnp.where(polar_mask, zero, horiz[step, 0, level])
                    w = jnp.where(polar_mask, zero, horiz[step, 1, level])
                    n = jnp.where(global_row == n_lat * lats - 1, zero, horiz[step, 2, level])
                    s = jnp.where(global_row == 0, zero, horiz[step, 3, level])
                    keep = 1.0 - e - w - n - s
                    edge = jnp.where(lane == lons - 1, e, jnp.where(lane == 0, w, zero))
                    e = jnp.where(lane == lons - 1, zero, e)
                    w = jnp.where(lane == 0, zero, w)
                    for t in range(count):
                        start = pl.multiple_of(self.base(t, level), 8)
                        here = padded[pl.ds(start, lats), :]
                        k = dl * count + t
                        field[self.tile(t, level), :] = (
                            keep * here
                            + e * pltpu.roll(here, lons - 1, 1)
                            + w * pltpu.roll(here, 1, 1)
                            + edge * pltpu.roll(halo, lons - 1 - 2 * k, 1)
                            + n * padded[pl.ds(start + 1, lats), :]
                            + s * padded[pl.ds(start - 1, lats), :]
                        )
                return carry

            lax.fori_loop(0, blocks, block, 0)

        def begin(self, step):
            self.vertical(step)
            self.release(step)
            self.pole_local(step)

        def end(self, step):
            self.receive(step)
            self.pole_finish(step)
            self.horizontal(step)

        def drain(self):
            for step in range(STEPS):
                for side in range(2):
                    self.row_copy(step, side).wait_send()
                    self.col_copy(step, side).wait_send()

                @pl.when(is_polar)
                def _():
                    for d in range(1, n_lon):
                        self.pole_copy(step, d).wait_send()

    def main(g):
        return Part(
            g * GROUP,
            GROUP,
            g,
            (
                lambda step, side: row_send.at[step, side, g],
                lambda step, side: row_recv.at[step, side, g],
                lambda step: col_send.at[step, g],
                lambda step, side: col_recv.at[step, side, g],
                lambda step: pole_send.at[step, g],
                lambda step: pole_recv.at[step, g],
                lambda step: pole_part.at[g],
            ),
        )

    extra = Part(
        tracers,
        1,
        groups,
        (
            lambda step, side: extra_row_send.at[step, side],
            lambda step, side: extra_row_recv.at[step, side],
            lambda step: extra_col_send.at[step],
            lambda step, side: extra_col_recv.at[step, side],
            lambda step: extra_pole_send.at[step],
            lambda step: extra_pole_recv.at[step],
            lambda step: extra_pole_part,
        ),
    )

    def over(lo, hi, body):
        def turn(g, carry):
            body(g)
            return carry

        lax.fori_loop(lo, hi, turn, 0)

    def out_copy(g):
        rows = pl.ds(pl.multiple_of(g * slab, slab), slab)
        return pltpu.make_async_copy(field.at[rows], out_hbm.at[rows], out_sem.at[g])

    def middle(g):
        part = main(g)
        part.end(1)
        part.begin(0)

    def last(g):
        main(g).end(0)
        out_copy(g).start()

    def first(g):
        load_slab(g).wait()
        main(g).begin(1)

    load_horiz.start()
    load_vert.wait()
    over(0, groups, first)
    forward()
    load_horiz.wait()
    over(0, groups, middle)
    collect()
    extra.begin(1)
    over(0, 1, last)
    extra.end(1)
    extra.begin(0)
    over(1, groups, last)
    extra.end(0)
    extra_copy = pltpu.make_async_copy(
        field.at[pl.ds(extra_base, levels * lats)], extra_hbm, out_sem.at[groups]
    )
    extra_copy.start()

    for d in range(1, n_lat):
        first_copy(d).wait_send()
    for d in range(1, n_lon):
        second_copy(d).wait_send()
    over(0, groups, lambda g: main(g).drain())
    extra.drain()
    over(0, groups, lambda g: out_copy(g).wait())
    extra_copy.wait()


def stay(array):
    return pltpu.with_memory_space_constraint(array, pltpu.HBM)


def transport(mesh_shape, adjoint_in, horiz_frac, vert_frac, shift, frac, sound, cols, counts):
    tracers, levels, lats, lons = adjoint_in.shape
    n_lat, n_lon = mesh_shape
    slots, senders = cols.shape
    groups = tracers // GROUP
    blocks = levels // BLOCK
    per_group = GROUP * levels
    features = sound.shape[1]
    f32 = jnp.float32
    any_spec = pl.BlockSpec(memory_space=pl.ANY)
    hbm = pl.BlockSpec(memory_space=pltpu.HBM)
    vmem = pl.BlockSpec(memory_space=pltpu.VMEM)
    smem = pl.BlockSpec(memory_space=pltpu.SMEM)
    dma = pltpu.SemaphoreType.DMA
    rows = tracers * levels * lats
    out, extra = pl.pallas_call(
        functools.partial(kernel, (tracers, levels, lats, lons, n_lat, n_lon, slots)),
        out_shape=(
            jax.ShapeDtypeStruct((rows, lons), f32),
            jax.ShapeDtypeStruct((levels * lats, lons), f32),
        ),
        in_specs=[smem, smem, hbm, hbm, hbm, hbm, vmem, vmem],
        out_specs=(any_spec, any_spec),
        scratch_shapes=[
            pltpu.VMEM((rows + levels * lats, lons), f32),
            pltpu.VMEM(horiz_frac.shape, f32),
            pltpu.VMEM(vert_frac.shape, f32),
            pltpu.VMEM(((tracers + 1) * levels * PITCH + 32, lons), f32),
            pltpu.VMEM((slots * senders, lons), jnp.int32),
            pltpu.VMEM((3 * (levels + 8), slots * senders), jnp.bfloat16),
            pltpu.VMEM((features, senders), f32),
            pltpu.VMEM((n_lat, n_lon, features), f32),
            pltpu.VMEM((senders * features // lons, lons), f32),
            pltpu.VMEM((senders * features // lons, lons), f32),
            pltpu.VMEM((STEPS, 2, groups, per_group, lons), f32),
            pltpu.VMEM((STEPS, 2, groups, per_group, lons), f32),
            pltpu.VMEM((STEPS, groups, blocks, lats, lons), f32),
            pltpu.VMEM((STEPS, 2, groups, blocks, lats, lons), f32),
            pltpu.VMEM((STEPS, groups, lats, lons), f32),
            pltpu.VMEM((STEPS, groups, n_lon, lats, lons), f32),
            pltpu.VMEM((groups, NPOLE, per_group, lons), f32),
            pltpu.VMEM((STEPS, 2, levels, lons), f32),
            pltpu.VMEM((STEPS, 2, levels, lons), f32),
            pltpu.VMEM((STEPS, blocks, lats, lons), f32),
            pltpu.VMEM((STEPS, 2, blocks, lats, lons), f32),
            pltpu.VMEM((STEPS, lats, lons), f32),
            pltpu.VMEM((STEPS, n_lon, lats, lons), f32),
            pltpu.VMEM((NPOLE, levels, lons), f32),
            pltpu.VMEM((STEPS, NPOLE, 3 * lons, lons), jnp.bfloat16),
            dma((3 + groups,)),
            dma((groups + 1,)),
            dma((n_lat,)),
            dma((n_lat,)),
            dma((n_lon,)),
            dma((n_lon,)),
            dma((STEPS, 2, groups + 1)),
            dma((STEPS, 2, groups + 1)),
            dma((STEPS, 2, groups + 1)),
            dma((STEPS, 2, groups + 1)),
            dma((STEPS, groups + 1, n_lon)),
            dma((STEPS, groups + 1, n_lon)),
        ],
        compiler_params=pltpu.CompilerParams(
            collective_id=0, has_side_effects=True, vmem_limit_bytes=VMEM_LIMIT
        ),
    )(
        stay(shift),
        stay(frac),
        stay(adjoint_in.reshape(rows, lons)),
        stay(horiz_frac),
        stay(vert_frac),
        stay(sound),
        stay(cols),
        stay(counts),
    )
    return out.reshape(adjoint_in.shape) + extra.reshape(levels, lats, lons)[None]


def solution(mesh):
    mesh_shape = (mesh.shape["lat"], mesh.shape["lon"])

    def on_device(
        adjoint_in,
        horiz_frac,
        vert_frac,
        polar_shift,
        polar_frac,
        sound_forcing,
        sound_col,
        sound_count,
    ):
        return transport(
            mesh_shape,
            adjoint_in,
            horiz_frac,
            vert_frac,
            polar_shift,
            polar_frac,
            sound_forcing[0],
            sound_col[0].T,
            sound_count,
        )

    return jax.shard_map(
        on_device,
        mesh=mesh,
        in_specs=(
            P(None, None, "lat", "lon"),
            P(None, None, None, "lat", "lon"),
            P(None, None, None, "lat", "lon"),
            P(),
            P(),
            P(("lat", "lon"), None, None),
            P(("lat", "lon"), None, None),
            P(("lat", "lon"), None),
        ),
        out_specs=P(None, None, "lat", "lon"),
        check_vma=False,
    )
```
